256 devices in a mesh: layer: 4 (over y_lo, core), phi: 64 (over y_hi, z, x).
Axes of the slice: x: 4, y: 4 (y_hi: 2, y_lo: 2; y = y_hi * 2 + y_lo), z: 8, core: 2. Of those that a mesh axis runs over, the one named last changes fastest.
Arguments:
- hit_features: bfloat16 [4, 64, 1024, 128], P('layer', 'phi'), may hold values from -6 to 6
- edge_features: bfloat16 [4, 64, 4, 1024, 128], P('layer', 'phi'), may hold values from -6 to 6
- sender_slot: int32 [4, 64, 4, 1024], P('layer', 'phi'), may hold values from 0 to 1023
- receiver_slot: int32 [4, 64, 4, 1024], P('layer', 'phi'), may hold values from 0 to 1023
- edge_count: int32 [4, 64, 4], P('layer', 'phi'), may hold values from 0 to 1024, as said below
- grad_hits: bfloat16 [4, 64, 1024, 128], P('layer', 'phi'), may hold values from -6 to 6
- grad_edges: bfloat16 [4, 64, 4, 1024, 128], P('layer', 'phi'), may hold values from -6 to 6
- w_edge_in: bfloat16 [384, 128], replicated, may hold values from -0.3125 to 0.3125
- w_edge_out: bfloat16 [128, 128], replicated, may hold values from -0.5 to 0.5
- w_node_in: bfloat16 [256, 128], replicated, may hold values from -0.375 to 0.375
- w_node_out: bfloat16 [128, 128], replicated, may hold values from -0.5 to 0.5
Outputs:
- hit_grads: float32 [4, 64, 1024, 128], P('layer', 'phi')
- edge_grads: bfloat16 [4, 64, 4, 1024, 128], P('layer', 'phi')
- edge_in_grad: float32 [384, 128], replicated
- edge_out_grad: float32 [128, 128], replicated
- node_in_grad: float32 [256, 128], replicated
- node_out_grad: float32 [128, 128], replicated
The draws below stay inside these ranges and needn't reach their ends.
Inputs may be any that keep to these rules, and one draw needn't show every extreme that they name: `edge_count`: live slots come first in each block. Kind 0 edges have their sender in the same shard, kind 1 in the previous layer group, kind 2 in the previous phi sector, kind 3 in the next one (phi closes into a loop). Kind 1 has no live slots in layer group 0. Some block is full in every draw. `sender_slot`: rows of dead slots are arbitrary. `receiver_slot`: rows of dead slots are arbitrary.
All inputs are finite; a program needn't handle non-finite values.
Results may differ from the reference program's by a relative error of at most 0.009.
Values may be sent and summed in bfloat16 or wider, within the bound.
A program may use at most 64 MiB of HBM per device.

```python
import jax
import jax.numpy as jnp
from jax import lax

D = 128
KINDS = 4
NODE_DEV = 1024
EDGE_CAP = 1024
LAYERS = 4
SECTORS = 64
SHARDS = 256


def draw_edge_count(key, part):
    level_key, jitter_key, chosen_key = jax.random.split(key, 3)
    grid_shape = (LAYERS, SECTORS, KINDS)
    levels = jax.random.randint(level_key, grid_shape, 0, 3).astype(jnp.int32)
    full_rows = jnp.right_shift(jnp.full(grid_shape, EDGE_CAP, jnp.int32), levels)
    jitter = jax.random.randint(jitter_key, grid_shape, 0, 1 << 20).astype(jnp.int32) % (full_rows // 4 + 1)
    counts = full_rows - jitter
    chosen = jax.random.randint(chosen_key, (), 0, LAYERS * SECTORS).astype(jnp.int32)
    device_flat = jnp.arange(LAYERS * SECTORS, dtype=jnp.int32).reshape(LAYERS, SECTORS, 1)
    kind_index = jnp.arange(KINDS, dtype=jnp.int32).reshape(1, 1, KINDS)
    layer_index = jnp.arange(LAYERS, dtype=jnp.int32).reshape(LAYERS, 1, 1)
    counts = jnp.where((device_flat == chosen) & (kind_index == 0), EDGE_CAP, counts)
    counts = jnp.where((layer_index == 0) & (kind_index == 1), 0, counts)
    return counts.astype(jnp.int32)


def place_ends(result, key, low, top_value):
    longest = result.shape.index(max(result.shape))
    spots = []
    for shift in (0, 1):
        where = [jax.random.randint(jax.random.fold_in(key, axis), (), 0, length) for axis, length in enumerate(result.shape)]
        where[longest] = (where[longest] + shift) % result.shape[longest]
        spots.append(tuple(where))
    return result.at[spots[0]].set(low).at[spots[1]].set(top_value)


def shard_levels(rng, shape, shards, smallest, high):
    loudness = 1.0
    for position, parts in shards:
        draws = jax.random.uniform(jax.random.fold_in(jax.random.fold_in(rng, 6), position), (parts,), jnp.float32, smallest / len(shards), high / len(shards))
        loudness = loudness * jnp.repeat(jnp.exp(draws), shape[position] // parts).reshape((-1,) + (1,) * (len(shape) - 1 - position))
    return loudness


def gaussian(key, dims, scale, bound, cuts=(), kind=jnp.bfloat16):
    entries = scale * jax.random.normal(key, dims, jnp.float32)
    if cuts:
        entries = entries * shard_levels(key, dims, cuts, -0.22, 0.18)
    return jnp.clip(entries, -bound, bound).astype(kind)


def setup_inputs(seed: int = 0) -> dict:
    keys = jax.random.split(jax.random.key(seed), 12)
    hit_features = gaussian(keys[0], (LAYERS, SECTORS, NODE_DEV, D), 1.0, 6.0, ((0, 4), (1, 64)))
    edge_features = gaussian(keys[1], (LAYERS, SECTORS, KINDS, EDGE_CAP, D), 1.0, 6.0, ((0, 4), (1, 64)))
    sender_slot = place_ends(jax.random.randint(keys[2], (LAYERS, SECTORS, KINDS, EDGE_CAP), 0, NODE_DEV), jax.random.fold_in(keys[2], 1), 0, NODE_DEV - 1).astype(jnp.int32)
    receiver_slot = place_ends(jax.random.randint(keys[3], (LAYERS, SECTORS, KINDS, EDGE_CAP), 0, NODE_DEV), jax.random.fold_in(keys[3], 1), 0, NODE_DEV - 1).astype(jnp.int32)
    edge_count = draw_edge_count(jax.random.fold_in(keys[11], 71), 0)
    grad_hits = gaussian(keys[5], (LAYERS, SECTORS, NODE_DEV, D), 1.0, 6.0, ((0, 4), (1, 64)))
    grad_edges = gaussian(keys[6], (LAYERS, SECTORS, KINDS, EDGE_CAP, D), 1.0, 6.0, ((0, 4), (1, 64)))
    w_edge_in = gaussian(keys[7], (3 * D, D), (3 * D) ** -0.5, 0.3125)
    w_edge_out = gaussian(keys[8], (D, D), D ** -0.5, 0.5)
    w_node_in = gaussian(keys[9], (2 * D, D), (2 * D) ** -0.5, 0.375)
    w_node_out = gaussian(keys[10], (D, D), D ** -0.5, 0.5)
    return {"hit_features": hit_features, "edge_features": edge_features, "sender_slot": sender_slot, "receiver_slot": receiver_slot, "edge_count": edge_count, "grad_hits": grad_hits, "grad_edges": grad_edges, "w_edge_in": w_edge_in, "w_edge_out": w_edge_out, "w_node_in": w_node_in, "w_node_out": w_node_out}


norm_eps = 1e-05

def norm_act(pre_act):
    average = lax.optimization_barrier(jnp.mean(pre_act, axis=-1, keepdims=True))
    centred = pre_act - average
    spread = lax.optimization_barrier(jnp.mean(centred * centred, axis=-1, keepdims=True))
    scaled = centred * lax.rsqrt(spread + norm_eps)
    return scaled * jax.nn.sigmoid(scaled)

def norm_act_back(pre_act, upstream):
    _, pullback = jax.vjp(norm_act, pre_act)
    return pullback(upstream)[0]

def reference(hit_features, edge_features, sender_slot, receiver_slot, edge_count, grad_hits, grad_edges, w_edge_in, w_edge_out, w_node_in, w_node_out):
    positions = jnp.arange(EDGE_CAP, dtype=jnp.int32)

    def locate(device_flat):
        layer_at = device_flat // SECTORS
        sector_at = device_flat % SECTORS
        prev_sector = (sector_at + SECTORS - 1) % SECTORS
        next_sector = (sector_at + 1) % SECTORS
        lower_layer = jnp.maximum(layer_at - 1, 0)
        has_lower = layer_at > 0
        local_rows = hit_features[layer_at, sector_at]
        lower_rows = jnp.where(has_lower, hit_features[lower_layer, sector_at], jnp.zeros_like(local_rows))
        sources = (local_rows, lower_rows, hit_features[layer_at, prev_sector], hit_features[layer_at, next_sector])
        targets = ((layer_at, sector_at), (lower_layer, sector_at), (layer_at, prev_sector), (layer_at, next_sector))
        live_mask = (positions[None, :] < edge_count[layer_at, sector_at][:, None]).astype(jnp.float32)
        return (layer_at, sector_at, sources, targets, has_lower, live_mask)

    def forward_kind(sources, k, send_idx, recv_idx, edge_rows):
        inputs = jnp.concatenate([jnp.take(sources[k], send_idx, axis=0), jnp.take(sources[0], recv_idx, axis=0), edge_rows], axis=-1)
        pre_act = jnp.dot(inputs, w_edge_in, preferred_element_type=jnp.float32)
        hidden = norm_act(pre_act).astype(jnp.bfloat16)
        return (inputs, pre_act, hidden)

    def device_incoming(device_flat):
        layer_at, sector_at, sources, targets, has_lower, live_mask = locate(device_flat)
        incoming = jnp.zeros((NODE_DEV, D), jnp.float32)
        for k in range(KINDS):
            send_idx = sender_slot[layer_at, sector_at, k]
            recv_idx = receiver_slot[layer_at, sector_at, k]
            _, _, hidden = forward_kind(sources, k, send_idx, recv_idx, edge_features[layer_at, sector_at, k])
            message = jnp.dot(hidden, w_edge_out, preferred_element_type=jnp.float32) * live_mask[k][:, None]
            incoming = incoming + jax.ops.segment_sum(message, recv_idx, num_segments=NODE_DEV)
        return incoming.astype(jnp.bfloat16)
    devices_all = jnp.arange(SHARDS, dtype=jnp.int32)
    incoming = lax.map(device_incoming, devices_all).reshape(LAYERS, SECTORS, NODE_DEV, D)
    node_in = jnp.concatenate([hit_features, incoming], axis=-1).reshape(SHARDS * NODE_DEV, 2 * D)
    node_pre = jnp.dot(node_in, w_node_in, preferred_element_type=jnp.float32)
    node_hidden = norm_act(node_pre).astype(jnp.bfloat16)
    grad_flat = grad_hits.reshape(SHARDS * NODE_DEV, D)
    node_hidden_grad = jnp.dot(grad_flat, w_node_out.T, preferred_element_type=jnp.float32)
    node_out_grad = jnp.dot(node_hidden.T, grad_flat, preferred_element_type=jnp.float32) / SHARDS
    node_pre_grad = norm_act_back(node_pre, node_hidden_grad).astype(jnp.bfloat16)
    node_input_grad = jnp.dot(node_pre_grad, w_node_in.T, preferred_element_type=jnp.float32)
    node_in_grad = jnp.dot(node_in.T, node_pre_grad, preferred_element_type=jnp.float32) / SHARDS
    incoming_grad = node_input_grad[:, D:].reshape(LAYERS, SECTORS, NODE_DEV, D)
    hit_start = (grad_flat.astype(jnp.float32) + node_input_grad[:, :D]).reshape(LAYERS, SECTORS, NODE_DEV, D)

    def device_back(totals, device_flat):
        hit_total, in_total, out_total = totals
        layer_at, sector_at, sources, targets, has_lower, live_mask = locate(device_flat)
        recv_total = jnp.zeros((NODE_DEV, D), jnp.float32)
        edge_list = []
        for k in range(KINDS):
            send_idx = sender_slot[layer_at, sector_at, k]
            recv_idx = receiver_slot[layer_at, sector_at, k]
            grad_rows = grad_edges[layer_at, sector_at, k]
            inputs, pre_act, hidden = forward_kind(sources, k, send_idx, recv_idx, edge_features[layer_at, sector_at, k])
            message_grad = (live_mask[k][:, None] * (grad_rows.astype(jnp.float32) + jnp.take(incoming_grad[layer_at, sector_at], recv_idx, axis=0))).astype(jnp.bfloat16)
            hidden_grad = jnp.dot(message_grad, w_edge_out.T, preferred_element_type=jnp.float32)
            out_total = out_total + jnp.dot(hidden.T, message_grad, preferred_element_type=jnp.float32)
            pre_grad = norm_act_back(pre_act, hidden_grad).astype(jnp.bfloat16)
            input_grad = jnp.dot(pre_grad, w_edge_in.T, preferred_element_type=jnp.float32)
            in_total = in_total + jnp.dot(inputs.T, pre_grad, preferred_element_type=jnp.float32)
            edge_list.append((grad_rows.astype(jnp.float32) + input_grad[:, 2 * D:]).astype(jnp.bfloat16))
            recv_total = recv_total + jax.ops.segment_sum(input_grad[:, D:2 * D], recv_idx, num_segments=NODE_DEV)
            send_total = jax.ops.segment_sum(input_grad[:, :D], send_idx, num_segments=NODE_DEV)
            if k == 1:
                send_total = send_total * has_lower.astype(jnp.float32)
            target_layer, target_sector = targets[k]
            hit_total = hit_total.at[target_layer, target_sector].add(send_total)
        hit_total = hit_total.at[layer_at, sector_at].add(recv_total)
        return ((hit_total, in_total, out_total), jnp.stack(edge_list))
    start_totals = (hit_start, jnp.zeros((3 * D, D), jnp.float32), jnp.zeros((D, D), jnp.float32))
    (hit_grads, in_total, out_total), edge_grads = lax.scan(device_back, start_totals, devices_all)
    edge_grads = edge_grads.reshape(LAYERS, SECTORS, KINDS, EDGE_CAP, D)
    return (hit_grads, edge_grads, in_total / SHARDS, out_total / SHARDS, node_in_grad, node_out_grad)
```

```python
import jax, jax.numpy as jnp, functools
from jax import lax
from jax.experimental import pallas as pl
from jax.experimental.pallas import tpu as pltpu
from jax.sharding import PartitionSpec as P
F32=jnp.float32; BF=jnp.bfloat16
N=1024; E=1024; D=128; K=4
TE=256

def mm(a,b): return jnp.dot(a,b,preferred_element_type=F32)
def mm_nt(a,b): return lax.dot_general(a,b,(((1,),(1,)),((),())),preferred_element_type=F32)
def mm_tn(a,b): return lax.dot_general(a,b,(((0,),(0,)),((),())),preferred_element_type=F32)
def halves(x):
    hi=x.astype(BF); lo=(x-hi.astype(F32)).astype(BF)
    return hi,lo
def put_halves(ref,x,rows=slice(None)):
    hi,lo=halves(x)
    ref[rows,0:D]=hi; ref[rows,D:2*D]=lo
def fold(x): return x[:,0:D]+x[:,D:2*D]

def gather_hot(dst, base, idx_row):
    col=jnp.broadcast_to(idx_row,(D,D)).T.astype(jnp.int16)
    lane=lax.broadcasted_iota(jnp.int16,(D,D),1)
    for j in range(N//D):
        dst[pl.ds(base,D), j*D:(j+1)*D]=jnp.where(col==lane+jnp.int16(j*D),BF(1),BF(0))

def norm_parts(pre):
    mean=jnp.mean(pre,axis=-1,keepdims=True)
    c=pre-mean
    var=jnp.mean(c*c,axis=-1,keepdims=True)
    r=lax.rsqrt(var+1e-5)
    u=c*r
    s=0.5+0.5*jnp.tanh(0.5*u)
    h=u*s
    return u,r,h,s+h*(1.0-s)

def norm_back(w,u):
    return w-jnp.mean(w,axis=-1,keepdims=True)-u*jnp.mean(w*u,axis=-1,keepdims=True)

def edge_kernel(cnt_ref, snd_ref, rcv_ref, hit_ref, s1_ref, s2_ref, s3_ref, ef_ref, gh_ref, ge_ref,
                wi_ref, wo_ref, ni_ref, no_ref,
                hit_out, b1_ref, b2_ref, b3_ref, edge_out, wg_ref,
                t1, t2, ohs, ohr, oht, A, U, hid, g, mg, si, ri):
    for k in range(K):
        for c in range(E//D):
            si[k,c:c+1,:]=snd_ref[k:k+1,c*D:(c+1)*D]
            ri[k,c:c+1,:]=rcv_ref[k:k+1,c*D:(c+1)*D]
    w1=wi_ref[0:D,:]; w2=wi_ref[D:2*D,:]; w3=wi_ref[2*D:3*D,:]
    srcs=(hit_ref,s1_ref,s2_ref,s3_ref)
    put_halves(t2, mm(hit_ref[...],w2))
    for k in range(K):
        put_halves(t1.at[k], mm(srcs[k][...],w1))
    def fwd(k,_):
        live_n=cnt_ref[k]
        for t in range(E//TE):
            row0=k*E+t*TE
            for c in range(TE//D):
                lo=t*TE+c*D
                gather_hot(ohs.at[t], c*D, si[k,lo//D:lo//D+1,:])
                gather_hot(ohr, pl.multiple_of(row0+c*D,D), ri[k,lo//D:lo//D+1,:])
            rows=pl.ds(pl.multiple_of(row0,TE),TE)
            acc=mm(ohs[t],t1[k])+mm(ohr[rows,:],t2[...])
            pre=fold(acc)+mm(ef_ref[rows,:],w3)
            u,r,h,d=norm_parts(pre)
            live=(lax.broadcasted_iota(jnp.int32,(TE,D),0)+t*TE)<live_n
            U[rows,:]=u
            A[rows,:]=jnp.where(live,r*d,0.0)
            hid[rows,:]=jnp.where(live,h,0.0).astype(BF)
        return 0
    lax.fori_loop(0,K,fwd,0)
    def hot_t(idx_ref,k,m):
        ids=idx_ref[k:k+1,:].astype(jnp.int16)
        io=lax.broadcasted_iota(jnp.int16,(TE,E),0)+(m*TE).astype(jnp.int16)
        return jnp.where(jnp.broadcast_to(ids,(TE,E))==io,BF(1),BF(0))
    def scat(m,_):
        rows=pl.ds(pl.multiple_of(m*TE,TE),TE)
        for k in range(K):
            oht[rows,k*E:(k+1)*E]=hot_t(rcv_ref,k,m)
        Hm=mm(oht[rows,:],hid[...])
        put_halves(t2,Hm,rows)
        return 0
    lax.fori_loop(0,N//TE,scat,0)
    wo=wo_ref[...]; wn1=ni_ref[0:D,:]; wn2=ni_ref[D:2*D,:]; no=no_ref[...]
    inc=(mm(t2[:,0:D],wo)+mm(t2[:,D:2*D],wo)).astype(BF)
    npre=mm(hit_ref[...],wn1)+mm(inc,wn2)
    u,r,h,d=norm_parts(npre)
    nh=h.astype(BF)
    gh=gh_ref[...]
    wg_ref[3*D+D+2*D:3*D+D+3*D,:]=mm_tn(nh,gh)
    w=mm_nt(gh,no)*(r*d)
    npg=norm_back(w,u).astype(BF)
    wg_ref[4*D:5*D,:]=mm_tn(hit_ref[...],npg)
    wg_ref[5*D:6*D,:]=mm_tn(inc,npg)
    hit_out[...]=gh.astype(F32)+mm_nt(npg,wn1)
    put_halves(t2,mm_nt(npg,wn2))
    def bwd(k,_):
        for t in range(E//TE):
            row0=k*E+t*TE
            rows=pl.ds(pl.multiple_of(row0,TE),TE)
            I=fold(mm(ohr[rows,:],t2[...]))
            gef=ge_ref[rows,:].astype(F32)
            m=(gef+I).astype(BF)
            mg[rows,:]=m
            dh=mm_nt(m,wo)
            gg=norm_back(dh*A[rows,:],U[rows,:]).astype(BF)
            g[rows,:]=gg
            edge_out[rows,:]=(gef+mm_nt(gg,w3)).astype(BF)
        return 0
    lax.fori_loop(0,K,bwd,0)
    wg_ref[3*D:4*D,:]=mm_tn(hid[...],mg[...])
    wg_ref[2*D:3*D,:]=mm_tn(ef_ref[...],g[...])
    def scat_r(m,_):
        rows=pl.ds(pl.multiple_of(m*TE,TE),TE)
        R=mm(oht[rows,:],g[...])
        put_halves(t2,R,rows)
        for k in range(K):
            S=mm(hot_t(snd_ref,k,m), g[k*E:(k+1)*E,:])
            put_halves(t1.at[k],S,rows)
        return 0
    lax.fori_loop(0,N//TE,scat_r,0)
    wg_ref[D:2*D,:]=fold(mm_tn(hit_ref[...],t2[...]))
    acc=mm_tn(hit_ref[...],t1[0])
    for k in range(1,K): acc=acc+mm_tn(srcs[k][...],t1[k])
    wg_ref[0:D,:]=fold(acc)
    wg_ref[7*D:8*D,:]=jnp.zeros((D,D),F32)
    def back(k): return mm_nt(t1[k,:,0:D],w1)+mm_nt(t1[k,:,D:2*D],w1)
    b1_ref[...]=back(1).astype(BF); b2_ref[...]=back(2).astype(BF); b3_ref[...]=back(3).astype(BF)
    hit_out[...]+=back(0)+mm_nt(t2[:,0:D],w2)+mm_nt(t2[:,D:2*D],w2)

def edge_call(cnt,snd,rcv,hit,s1,s2,s3,ef,gh,ge,wi,wo,ni,no):
    V=pl.BlockSpec(memory_space=pltpu.VMEM)
    return pl.pallas_call(edge_kernel,
        out_shape=(jax.ShapeDtypeStruct((N,D),F32),)+(jax.ShapeDtypeStruct((N,D),BF),)*3+(jax.ShapeDtypeStruct((K*E,D),BF),jax.ShapeDtypeStruct((8*D,D),F32)),
        in_specs=[pl.BlockSpec(memory_space=pltpu.SMEM)]+[V]*13,
        out_specs=(V,)*6,
        scratch_shapes=[pltpu.VMEM((K,N,2*D),BF),pltpu.VMEM((N,2*D),BF),pltpu.VMEM((E//TE,TE,N),BF),
            pltpu.VMEM((K*E,N),BF),pltpu.VMEM((N,K*E),BF),pltpu.VMEM((K*E,D),F32),pltpu.VMEM((K*E,D),F32),
            pltpu.VMEM((K*E,D),BF),pltpu.VMEM((K*E,D),BF),pltpu.VMEM((K*E,D),BF),pltpu.VMEM((K,E//D,D),jnp.int32),pltpu.VMEM((K,E//D,D),jnp.int32)],
        compiler_params=pltpu.CompilerParams(vmem_limit_bytes=60<<20),
        name="edge_step",
    )(cnt,snd,rcv,hit,s1,s2,s3,ef,gh,ge,wi,wo,ni,no)


MESH = pl.DeviceIdType.MESH
LX, LZ, LC = 4, 8, 2
XY = 16
HALF = 512
PIECE = HALF // XY


def place():
    layer = lax.axis_index("layer")
    phi = lax.axis_index("phi")
    core = layer % 2
    spot = ((phi // 32) * 2 + layer // 2) * 4 + phi % 4
    z = (phi // 4) % 8
    return core, spot, z


def device_at(core, spot, z):
    y = spot // 4
    return ((y % 2) * 2 + core, (y // 2) * 32 + z * 4 + spot % 4)


def reduce_kernel(x_ref, fin, send_a, recv_a, send_b, recv_b, recv_c, send_c, send_d,
                  sem_s, sem_r):
    core, spot, z = place()
    mate = device_at(1 - core, spot, z)
    plane = [device_at(core, (spot + d) % XY, z) for d in range(1, XY)]
    line = [device_at(core, spot, (z + d) % LZ) for d in range(1, LZ)]
    barrier = pltpu.get_barrier_semaphore()
    for other in [mate] + plane + line:
        pl.semaphore_signal(barrier, inc=1, device_id=other, device_id_type=MESH)
    mine = pl.multiple_of(core * HALF, HALF)
    theirs = pl.multiple_of((1 - core) * HALF, HALF)
    send_a[...] = x_ref[pl.ds(theirs, HALF), :].astype(BF)
    pl.semaphore_wait(barrier, len(plane) + len(line) + 1)

    def remote(src, dst, n, to):
        return pltpu.make_async_remote_copy(
            src_ref=src, dst_ref=dst, send_sem=sem_s.at[n], recv_sem=sem_r.at[n],
            device_id=to, device_id_type=MESH)

    first = remote(send_a, recv_a, 0, mate)
    first.start()
    first.wait()
    half = x_ref[pl.ds(mine, HALF), :] + recv_a[...].astype(F32)
    send_b[...] = half.astype(BF)
    copies = []
    for d, other in enumerate(plane, 1):
        to = pl.multiple_of(((spot + d) % XY) * PIECE, PIECE)
        copies.append(remote(send_b.at[pl.ds(to, PIECE), :], recv_b.at[spot], d, other))
        copies[-1].start()
    recv_b[spot] = send_b[pl.ds(pl.multiple_of(spot * PIECE, PIECE), PIECE), :]
    for c in copies:
        c.wait()
    total = recv_b[0].astype(F32)
    for j in range(1, XY):
        total = total + recv_b[j].astype(F32)
    send_c[...] = total.astype(BF)
    copies = []
    for d, other in enumerate(line, 1):
        copies.append(remote(send_c, recv_c.at[z], XY + d, other))
        copies[-1].start()
    recv_c[z] = send_c[...]
    for c in copies:
        c.wait()
    total = recv_c[0].astype(F32)
    for j in range(1, LZ):
        total = total + recv_c[j].astype(F32)
    send_d[...] = (total * (1.0 / 256.0)).astype(BF)
    here = pl.ds(pl.multiple_of(core * HALF + spot * PIECE, PIECE), PIECE)
    copies = []
    for d, other in enumerate(plane, 1):
        copies.append(remote(send_d, fin.at[here, :], XY + LZ + d, other))
        copies[-1].start()
    fin[here, :] = send_d[...]
    for c in copies:
        c.wait()
    half_rows = pl.ds(mine, HALF)
    last = remote(fin.at[half_rows, :], fin.at[half_rows, :], XY + LZ, mate)
    last.start()
    last.wait()


def reduce_call(x):
    return pl.pallas_call(
        reduce_kernel,
        out_shape=jax.ShapeDtypeStruct((2 * HALF, D), BF),
        in_specs=[pl.BlockSpec(memory_space=pltpu.VMEM)],
        out_specs=pl.BlockSpec(memory_space=pltpu.VMEM),
        scratch_shapes=[
            pltpu.VMEM((HALF, D), BF), pltpu.VMEM((HALF, D), BF),
            pltpu.VMEM((HALF, D), BF), pltpu.VMEM((XY, PIECE, D), BF),
            pltpu.VMEM((LZ, PIECE, D), BF), pltpu.VMEM((PIECE, D), BF), pltpu.VMEM((PIECE, D), BF),
            pltpu.SemaphoreType.DMA((2 * XY + LZ,)),
            pltpu.SemaphoreType.DMA((2 * XY + LZ,)),
        ],
        compiler_params=pltpu.CompilerParams(collective_id=0, has_side_effects=True),
        name="weight_sum",
    )(x)


def shifted(value, axis, steps, wrap):
    count = lax.axis_size(axis)
    if wrap:
        pairs = [(i, (i + steps) % count) for i in range(count)]
    else:
        pairs = [(i, i + steps) for i in range(count) if 0 <= i + steps < count]
    return lax.ppermute(value, axis, pairs)


def body(hit, ef, snd, rcv, cnt, gh, ge, wi, wo, ni, no):
    rows = hit[0, 0]
    s1 = shifted(rows, "layer", 1, False)
    s2 = shifted(rows, "phi", 1, True)
    s3 = shifted(rows, "phi", -1, True)
    local, b1, b2, b3, edges, parts = edge_call(
        cnt[0, 0], snd[0, 0], rcv[0, 0], rows, s1, s2, s3, ef[0, 0].reshape(K * E, D),
        gh[0, 0], ge[0, 0].reshape(K * E, D), wi, wo, ni, no)
    r1 = shifted(b1, "layer", -1, False)
    r2 = shifted(b2, "phi", -1, True)
    r3 = shifted(b3, "phi", 1, True)
    fin = reduce_call(parts)
    hits = local + r1.astype(F32) + r2.astype(F32) + r3.astype(F32)
    w = fin.astype(F32)
    return (hits[None, None], edges.reshape(1, 1, K, E, D),
            w[0:384], w[384:512], w[512:768], w[768:896])


def solution(mesh):
    two = P("layer", "phi", None, None)
    three = P("layer", "phi", None, None, None)
    return jax.shard_map(
        body, mesh=mesh,
        in_specs=(two, three, two, two, P("layer", "phi", None), two, three, P(), P(), P(), P()),
        out_specs=(two, three, P(), P(), P(), P()),
        check_vma=False,
    )
```

```python
import jax
import jax.numpy as jnp
from jax import lax
from jax.experimental import pallas as pl
from jax.experimental.pallas import tpu as pltpu
from jax.sharding import PartitionSpec as P

F32 = jnp.float32
BF = jnp.bfloat16
MESH = pl.DeviceIdType.MESH
N, E, D, K = 1024, 1024, 128, 4
KE = K * E
TE = 256
LZ, XY, HALF = 8, 16, 512
PIECE = HALF // XY


def mm(a, b):
    return jnp.dot(a, b, preferred_element_type=F32)


def mm_nt(a, b):
    return lax.dot_general(a, b, (((1,), (1,)), ((), ())), preferred_element_type=F32)


def mm_tn(a, b):
    return lax.dot_general(a, b, (((0,), (0,)), ((), ())), preferred_element_type=F32)


def halves(x):
    hi = x.astype(BF)
    return hi, (x - hi.astype(F32)).astype(BF)


def wide_nt(x, w):
    hi, lo = halves(x)
    return mm_nt(hi, w) + mm_nt(lo, w)


def fold(x):
    return x[:, 0:D] + x[:, D:2 * D]


def gather_hot(dst, base, idx_row):
    col = jnp.broadcast_to(idx_row, (D, D)).T.astype(jnp.int16)
    lane = lax.broadcasted_iota(jnp.int16, (D, D), 1)
    for j in range(N // D):
        dst[pl.ds(base, D), j * D:(j + 1) * D] = jnp.where(
            col == lane + jnp.int16(j * D), BF(1), BF(0))


def scatter_hot(idx_ref, k, m):
    ids = idx_ref[k:k + 1, :].astype(jnp.int16)
    io = lax.broadcasted_iota(jnp.int16, (TE, E), 0) + (m * TE).astype(jnp.int16)
    return jnp.where(jnp.broadcast_to(ids, (TE, E)) == io, BF(1), BF(0))


def norm_parts(pre):
    mean = jnp.mean(pre, axis=-1, keepdims=True)
    c = pre - mean
    var = jnp.mean(c * c, axis=-1, keepdims=True)
    r = lax.rsqrt(var + 1e-5)
    u = c * r
    s = 0.5 + 0.5 * jnp.tanh(0.5 * u)
    h = u * s
    return u, h, r * (s + h * (1.0 - s))


def norm_back(w, u):
    return w - jnp.mean(w, axis=-1, keepdims=True) - u * jnp.mean(w * u, axis=-1, keepdims=True)


def rows_at(start, size):
    return pl.ds(pl.multiple_of(start, size), size)


def step_kernel(cnt_ref, snd_ref, rcv_ref, hit_any, ef_any, gh_any, ge_any,
                wi_ref, wo_ref, ni_ref, no_ref,
                hit_out, edge_out, fin,
                src, inp, gh, ge, ohs, ohr, oht, A, U, hid, g, mg, t3, si, ri, wg,
                bsend, brecv, send_a, recv_a, send_b, recv_b, recv_c, send_c, send_d,
                sem_in, sem_hs, sem_hr, sem_s, sem_r):
    layer = lax.axis_index("layer")
    phi = lax.axis_index("phi")
    core = layer % 2
    spot = ((phi // 32) * 2 + layer // 2) * 4 + phi % 4
    z = (phi // 4) % 8

    def at(c, s, zz):
        y = s // 4
        return ((y % 2) * 2 + c, (y // 2) * 32 + zz * 4 + s % 4)

    up = ((layer + 1) % 4, phi)
    down = ((layer + 3) % 4, phi)
    after = (layer, (phi + 1) % 64)
    before = (layer, (phi + 63) % 64)
    mate = at(1 - core, spot, z)
    plane = [at(core, (spot + d) % XY, z) for d in range(1, XY)]
    line = [at(core, spot, (z + d) % LZ) for d in range(1, LZ)]
    everyone = [up, down, after, before, mate] + plane + line
    barrier = pltpu.get_barrier_semaphore()
    for other in everyone:
        pl.semaphore_signal(barrier, inc=1, device_id=other, device_id_type=MESH)
    loads = [
        pltpu.make_async_copy(hit_any, src.at[0], sem_in.at[0]),
        pltpu.make_async_copy(ef_any, inp.at[:, 2 * D:3 * D], sem_in.at[1]),
        pltpu.make_async_copy(gh_any, gh, sem_in.at[2]),
        pltpu.make_async_copy(ge_any, ge, sem_in.at[3]),
    ]
    for c in loads:
        c.start()
    for k in range(K):
        for c in range(E // D):
            si[k, c:c + 1, :] = snd_ref[k:k + 1, c * D:(c + 1) * D]
            ri[k, c:c + 1, :] = rcv_ref[k:k + 1, c * D:(c + 1) * D]
    loads[0].wait()
    pl.semaphore_wait(barrier, len(everyone))

    def halo(s, d, n, to):
        return pltpu.make_async_remote_copy(
            src_ref=s, dst_ref=d, send_sem=sem_hs.at[n], recv_sem=sem_hr.at[n],
            device_id=to, device_id_type=MESH)

    def remote(s, d, n, to):
        return pltpu.make_async_remote_copy(
            src_ref=s, dst_ref=d, send_sem=sem_s.at[n], recv_sem=sem_r.at[n],
            device_id=to, device_id_type=MESH)

    outward = [halo(src.at[0], src.at[1], 0, up), halo(src.at[0], src.at[2], 1, after),
               halo(src.at[0], src.at[3], 2, before)]
    for c in outward:
        c.start()

    wi = wi_ref[...]
    w1, w2, w3 = wi[0:D, :], wi[D:2 * D, :], wi[2 * D:3 * D, :]
    wo = wo_ref[...]
    wn1, wn2 = ni_ref[0:D, :], ni_ref[D:2 * D, :]

    def receivers(k, _):
        for t in range(E // TE):
            for c in range(TE // D):
                n = t * (TE // D) + c
                gather_hot(ohr, pl.multiple_of(k * E + n * D, D), ri[k, n:n + 1, :])
            rows = rows_at(k * E + t * TE, TE)
            inp[rows, D:2 * D] = mm(ohr[rows, :], src[0]).astype(BF)
        return 0

    lax.fori_loop(0, K, receivers, 0)
    loads[1].wait()

    def forward(k, _):
        count = cnt_ref[k]
        for t in range(E // TE):
            for c in range(TE // D):
                n = t * (TE // D) + c
                gather_hot(ohs.at[t], c * D, si[k, n:n + 1, :])
            rows = rows_at(k * E + t * TE, TE)
            inp[rows, 0:D] = mm(ohs[t], src[k]).astype(BF)
            u, h, d = norm_parts(mm(inp[rows, :], wi))
            live = (lax.broadcasted_iota(jnp.int32, (TE, D), 0) + t * TE) < count
            U[rows, :] = u
            A[rows, :] = jnp.where(live, d, 0.0)
            hid[rows, :] = jnp.where(live, h, 0.0).astype(BF)
        return 0

    forward(0, 0)
    for c in outward:
        c.wait()
    lax.fori_loop(1, K, forward, 0)

    def collect(m, _):
        rows = rows_at(m * TE, TE)
        for k in range(K):
            oht[rows, k * E:(k + 1) * E] = scatter_hot(rcv_ref, k, m)
        hi, lo = halves(mm(oht[rows, :], hid[...]))
        t3[rows, 0:D] = hi
        t3[rows, D:2 * D] = lo
        return 0

    lax.fori_loop(0, N // TE, collect, 0)
    loads[2].wait()
    incoming = (mm(t3[:, 0:D], wo) + mm(t3[:, D:2 * D], wo)).astype(BF)
    u, h, d = norm_parts(mm(src[0], wn1) + mm(incoming, wn2))
    ghv = gh[...]
    wg[6 * D:7 * D, :] = mm_tn(h.astype(BF), ghv)
    npg = norm_back(mm_nt(ghv, no_ref[...]) * d, u).astype(BF)
    wg[4 * D:5 * D, :] = mm_tn(src[0], npg)
    wg[5 * D:6 * D, :] = mm_tn(incoming, npg)
    wg[7 * D:8 * D, :] = jnp.zeros((D, D), F32)
    wg[0:4 * D, :] = jnp.zeros((4 * D, D), F32)
    hit_out[...] = ghv.astype(F32) + mm_nt(npg, wn1)
    hi, lo = halves(mm_nt(npg, wn2))
    t3[:, 0:D] = hi
    t3[:, D:2 * D] = lo
    loads[3].wait()

    def backward(k, _):
        for t in range(E // TE):
            rows = rows_at(k * E + t * TE, TE)
            m = (ge[rows, :].astype(F32) + fold(mm(ohr[rows, :], t3[...]))).astype(BF)
            mg[rows, :] = m
            g[rows, :] = norm_back(mm_nt(m, wo) * A[rows, :], U[rows, :]).astype(BF)
        rows = rows_at(k * E, E)
        wg[0:3 * D, :] += mm_tn(inp[rows, :], g[rows, :])
        wg[3 * D:4 * D, :] += mm_tn(hid[rows, :], mg[rows, :])
        return 0

    lax.fori_loop(0, K, backward, 0)

    mine = rows_at(core * HALF, HALF)
    send_a[...] = wg[rows_at((1 - core) * HALF, HALF), :].astype(BF)
    first = remote(send_a, recv_a, 0, mate)
    first.start()

    def give_back(k):
        def part(m, _):
            rows = rows_at(m * TE, TE)
            s = mm(scatter_hot(snd_ref, k, m), g[k * E:(k + 1) * E, :])
            bsend[k - 1, rows, :] = wide_nt(s, w1).astype(BF)
            return 0
        lax.fori_loop(0, N // TE, part, 0)
        c = halo(bsend.at[k - 1], brecv.at[k - 1], 2 + k, (None, down, before, after)[k])
        c.start()
        return c

    homeward = [give_back(2)]
    first.wait()
    send_b[...] = (wg[mine, :] + recv_a[...].astype(F32)).astype(BF)
    copies = []
    for d, other in enumerate(plane, 1):
        copies.append(remote(send_b.at[rows_at(((spot + d) % XY) * PIECE, PIECE), :],
                             recv_b.at[spot], d, other))
        copies[-1].start()
    recv_b[spot] = send_b[rows_at(spot * PIECE, PIECE), :]
    homeward.append(give_back(3))
    homeward.append(give_back(1))
    for c in copies:
        c.wait()
    total = recv_b[0].astype(F32)
    for j in range(1, XY):
        total = total + recv_b[j].astype(F32)
    send_c[...] = total.astype(BF)
    copies = []
    for d, other in enumerate(line, 1):
        copies.append(remote(send_c, recv_c.at[z], XY + d, other))
        copies[-1].start()
    recv_c[z] = send_c[...]

    def own_part(m, _):
        rows = rows_at(m * TE, TE)
        s = mm(scatter_hot(snd_ref, 0, m), g[0:E, :])
        r = mm(oht[rows, :], g[...])
        hit_out[rows, :] += wide_nt(s, w1) + wide_nt(r, w2)
        return 0

    lax.fori_loop(0, N // TE, own_part, 0)
    for c in copies:
        c.wait()
    total = recv_c[0].astype(F32)
    for j in range(1, LZ):
        total = total + recv_c[j].astype(F32)
    send_d[...] = (total * (1.0 / 256.0)).astype(BF)
    here = rows_at(core * HALF + spot * PIECE, PIECE)
    copies = []
    for d, other in enumerate(plane, 1):
        copies.append(remote(send_d, fin.at[here, :], XY + LZ + d, other))
        copies[-1].start()
    fin[here, :] = send_d[...]

    def edges(n, _):
        rows = rows_at(n * TE, TE)
        edge_out[rows, :] = (ge[rows, :].astype(F32) + mm_nt(g[rows, :], w3)).astype(BF)
        return 0

    lax.fori_loop(0, KE // TE, edges, 0)
    for c in copies:
        c.wait()
    last = remote(fin.at[mine, :], fin.at[mine, :], XY + LZ, mate)
    last.start()
    for c in homeward:
        c.wait()
    hit_out[...] += (brecv[0].astype(F32) + brecv[1].astype(F32)) + brecv[2].astype(F32)
    last.wait()


def step_call(cnt, snd, rcv, hit, ef, gh, ge, wi, wo, ni, no):
    V = pl.BlockSpec(memory_space=pltpu.VMEM)
    H = pl.BlockSpec(memory_space=pl.ANY)
    sem = pltpu.SemaphoreType.DMA
    return pl.pallas_call(
        step_kernel,
        out_shape=(jax.ShapeDtypeStruct((N, D), F32), jax.ShapeDtypeStruct((KE, D), BF),
                   jax.ShapeDtypeStruct((8 * D, D), BF)),
        in_specs=[pl.BlockSpec(memory_space=pltpu.SMEM), V, V, H, H, H, H, V, V, V, V],
        out_specs=(V, V, V),
        scratch_shapes=[
            pltpu.VMEM((K, N, D), BF), pltpu.VMEM((KE, 3 * D), BF),
            pltpu.VMEM((N, D), BF), pltpu.VMEM((KE, D), BF),
            pltpu.VMEM((E // TE, TE, N), BF), pltpu.VMEM((KE, N), BF), pltpu.VMEM((N, KE), BF),
            pltpu.VMEM((KE, D), F32), pltpu.VMEM((KE, D), F32), pltpu.VMEM((KE, D), BF),
            pltpu.VMEM((KE, D), BF), pltpu.VMEM((KE, D), BF), pltpu.VMEM((N, 2 * D), BF),
            pltpu.VMEM((K, E // D, D), jnp.int32), pltpu.VMEM((K, E // D, D), jnp.int32),
            pltpu.VMEM((8 * D, D), F32),
            pltpu.VMEM((3, N, D), BF), pltpu.VMEM((3, N, D), BF),
            pltpu.VMEM((HALF, D), BF), pltpu.VMEM((HALF, D), BF), pltpu.VMEM((HALF, D), BF),
            pltpu.VMEM((XY, PIECE, D), BF), pltpu.VMEM((LZ, PIECE, D), BF),
            pltpu.VMEM((PIECE, D), BF), pltpu.VMEM((PIECE, D), BF),
            sem((4,)), sem((6,)), sem((6,)), sem((2 * XY + LZ,)), sem((2 * XY + LZ,)),
        ],
        compiler_params=pltpu.CompilerParams(
            vmem_limit_bytes=60 << 20, collective_id=0, has_side_effects=True),
        name="graph_step",
    )(cnt, snd, rcv, hit, ef, gh, ge, wi, wo, ni, no)


def body(hit, ef, snd, rcv, cnt, gh, ge, wi, wo, ni, no):
    hits, edges, fin = step_call(
        cnt[0, 0], snd[0, 0], rcv[0, 0], hit[0, 0], ef[0, 0].reshape(KE, D),
        gh[0, 0], ge[0, 0].reshape(KE, D), wi, wo, ni, no)
    w = fin.astype(F32)
    return (hits[None, None], edges.reshape(1, 1, K, E, D),
            w[0:384], w[384:512], w[512:768], w[768:896])


def solution(mesh):
    two = P("layer", "phi", None, None)
    three = P("layer", "phi", None, None, None)
    return jax.shard_map(
        body, mesh=mesh,
        in_specs=(two, three, two, two, P("layer", "phi", None), two, three, P(), P(), P(), P()),
        out_specs=(two, three, P(), P(), P(), P()),
        check_vma=False,
    )
```

```python
import jax
import jax.numpy as jnp
from jax import lax
from jax.experimental import pallas as pl
from jax.experimental.pallas import tpu as pltpu
from jax.sharding import PartitionSpec as P

F32 = jnp.float32
BF = jnp.bfloat16
MESH = pl.DeviceIdType.MESH
N, E, D, K = 1024, 1024, 128, 4
KE = K * E
TE = 256
LZ, XY, HALF = 8, 16, 512
PIECE = HALF // XY


def mm(a, b):
    return jnp.dot(a, b, preferred_element_type=F32)


def mm2(a, b):
    return jnp.dot(a, jnp.concatenate([b, b], axis=1), preferred_element_type=F32)[:, 0:D]


def mm_nt(a, b):
    return lax.dot_general(a, b, (((1,), (1,)), ((), ())), preferred_element_type=F32)


def mm_tn(a, b):
    return lax.dot_general(a, b, (((0,), (0,)), ((), ())), preferred_element_type=F32)


def halves(x):
    hi = x.astype(BF)
    return hi, (x - hi.astype(F32)).astype(BF)


def wide_nt(x, w):
    hi, lo = halves(x)
    return mm_nt(hi, w) + mm_nt(lo, w)


def fold(x):
    return x[:, 0:D] + x[:, D:2 * D]


def gather_hot(col):
    lane = lax.broadcasted_iota(jnp.int16, (D, D), 1)
    return jnp.concatenate(
        [jnp.where(col == lane + jnp.int16(j * D), BF(1), BF(0)) for j in range(N // D)], axis=1)


def spread(idx_row):
    return jnp.broadcast_to(idx_row, (D, D)).T.astype(jnp.int16)


def scatter_hot(idx_ref, k, m):
    ids = idx_ref[k:k + 1, :].astype(jnp.int16)
    io = lax.broadcasted_iota(jnp.int16, (TE, E), 0) + (m * TE).astype(jnp.int16)
    return jnp.where(jnp.broadcast_to(ids, (TE, E)) == io, BF(1), BF(0))


def norm_parts(pre):
    mean = jnp.mean(pre, axis=-1, keepdims=True)
    c = pre - mean
    var = jnp.mean(c * c, axis=-1, keepdims=True)
    r = lax.rsqrt(var + 1e-5)
    u = c * r
    s = 0.5 + 0.5 * jnp.tanh(0.5 * u)
    h = u * s
    return u, h, r * (s + h * (1.0 - s))


def norm_back(w, u):
    return w - jnp.mean(w, axis=-1, keepdims=True) - u * jnp.mean(w * u, axis=-1, keepdims=True)


def rows_at(start, size):
    return pl.ds(pl.multiple_of(start, size), size)


def step_kernel(cnt_ref, snd_ref, rcv_ref, hit_any, ef_any, gh_any, ge_any,
                wi_ref, wo_ref, ni_ref, no_ref,
                hit_out, edge_out, fin,
                src, inp, gh, ge, rcol, oht, wt, ebuf, A, U, hid, g, mg, t3, si, ri, wg,
                bsend, brecv, send_a, recv_a, send_b, recv_b, recv_c, send_c, send_d,
                sem_in, sem_hs, sem_hr, sem_s, sem_r):
    layer = lax.axis_index("layer")
    phi = lax.axis_index("phi")
    core = layer % 2
    spot = ((phi // 32) * 2 + layer // 2) * 4 + phi % 4
    z = (phi // 4) % 8

    def at(c, s, zz):
        y = s // 4
        return ((y % 2) * 2 + c, (y // 2) * 32 + zz * 4 + s % 4)

    up = ((layer + 1) % 4, phi)
    down = ((layer + 3) % 4, phi)
    after = (layer, (phi + 1) % 64)
    before = (layer, (phi + 63) % 64)
    mate = at(1 - core, spot, z)
    plane = [at(core, (spot + d) % XY, z) for d in range(1, XY)]
    line = [at(core, spot, (z + d) % LZ) for d in range(1, LZ)]
    everyone = [up, down, after, before, mate] + plane + line
    barrier = pltpu.get_barrier_semaphore()
    for other in everyone:
        pl.semaphore_signal(barrier, inc=1, device_id=other, device_id_type=MESH)
    loads = [
        pltpu.make_async_copy(hit_any, src.at[0], sem_in.at[0]),
        pltpu.make_async_copy(ef_any, inp.at[:, 2 * D:3 * D], sem_in.at[1]),
        pltpu.make_async_copy(gh_any, gh, sem_in.at[2]),
        pltpu.make_async_copy(ge_any, ge, sem_in.at[3]),
    ]
    for c in loads:
        c.start()
    for k in range(K):
        for c in range(E // D):
            si[k, c:c + 1, :] = snd_ref[k:k + 1, c * D:(c + 1) * D]
            ri[k, c:c + 1, :] = rcv_ref[k:k + 1, c * D:(c + 1) * D]
    loads[0].wait()
    pl.semaphore_wait(barrier, len(everyone))

    def halo(s, d, n, to):
        return pltpu.make_async_remote_copy(
            src_ref=s, dst_ref=d, send_sem=sem_hs.at[n], recv_sem=sem_hr.at[n],
            device_id=to, device_id_type=MESH)

    def remote(s, d, n, to):
        return pltpu.make_async_remote_copy(
            src_ref=s, dst_ref=d, send_sem=sem_s.at[n], recv_sem=sem_r.at[n],
            device_id=to, device_id_type=MESH)

    outward = [halo(src.at[0], src.at[1], 0, up), halo(src.at[0], src.at[2], 1, after),
               halo(src.at[0], src.at[3], 2, before)]
    for c in outward:
        c.start()

    wi = wi_ref[...]
    w1, w2, w3 = wi[0:D, :], wi[D:2 * D, :], wi[2 * D:3 * D, :]
    wo = wo_ref[...]
    wn1, wn2 = ni_ref[0:D, :], ni_ref[D:2 * D, :]

    def receivers(k, _):
        for n in range(E // D):
            rows = rows_at(k * E + n * D, D)
            col = spread(ri[k, n:n + 1, :])
            rcol[rows, :] = col
            inp[rows, D:2 * D] = mm2(gather_hot(col), src[0]).astype(BF)
        return 0

    lax.fori_loop(0, K, receivers, 0)
    loads[1].wait()

    def forward(k, _):
        count = cnt_ref[k]
        for n in range(E // D):
            rows = rows_at(k * E + n * D, D)
            inp[rows, 0:D] = mm2(gather_hot(spread(si[k, n:n + 1, :])), src[k]).astype(BF)
        for t in range(E // TE):
            rows = rows_at(k * E + t * TE, TE)
            u, h, d = norm_parts(mm2(inp[rows, :], wi))
            live = (lax.broadcasted_iota(jnp.int32, (TE, D), 0) + t * TE) < count
            U[rows, :] = u
            A[rows, :] = jnp.where(live, d, 0.0)
            hid[rows, :] = jnp.where(live, h, 0.0).astype(BF)
        return 0

    forward(0, 0)
    for k in range(1, K):
        outward[k - 1].wait()
        forward(k, 0)

    def collect(m, _):
        rows = rows_at(m * TE, TE)
        for k in range(K):
            oht[rows, k * E:(k + 1) * E] = scatter_hot(rcv_ref, k, m)
        hi, lo = halves(mm2(oht[rows, :], hid[...]))
        t3[rows, 0:D] = hi
        t3[rows, D:2 * D] = lo
        return 0

    lax.fori_loop(0, N // TE, collect, 0)
    loads[2].wait()
    incoming = (mm(t3[:, 0:D], wo) + mm(t3[:, D:2 * D], wo)).astype(BF)
    u, h, d = norm_parts(mm(src[0], wn1) + mm(incoming, wn2))
    ghv = gh[...]
    wg[6 * D:7 * D, :] = mm_tn(h.astype(BF), ghv)
    npg = norm_back(mm_nt(ghv, no_ref[...]) * d, u).astype(BF)
    wg[4 * D:5 * D, :] = mm_tn(src[0], npg)
    wg[5 * D:6 * D, :] = mm_tn(incoming, npg)
    wg[7 * D:8 * D, :] = jnp.zeros((D, D), F32)
    wt[...] = jnp.zeros((D, 4 * D), F32)
    hit_out[...] = ghv.astype(F32) + mm_nt(npg, wn1)
    hi, lo = halves(mm_nt(npg, wn2))
    t3[:, 0:D] = hi
    t3[:, D:2 * D] = lo
    loads[3].wait()

    def backward(k, _):
        for n in range(E // D):
            rows = rows_at(k * E + n * D, D)
            mg[rows, :] = (ge[rows, :].astype(F32)
                           + fold(mm(gather_hot(rcol[rows, :]), t3[...]))).astype(BF)
        for t in range(E // TE):
            rows = rows_at(k * E + t * TE, TE)
            g[rows, :] = norm_back(mm_nt(mg[rows, :], wo) * A[rows, :], U[rows, :]).astype(BF)
        rows = rows_at(k * E, E)
        wt[:, 0:3 * D] += mm_tn(g[rows, :], inp[rows, :])
        wt[:, 3 * D:4 * D] += mm_tn(mg[rows, :], hid[rows, :])
        return 0

    lax.fori_loop(0, K, backward, 0)
    for j in range(4):
        wg[j * D:(j + 1) * D, :] = wt[:, j * D:(j + 1) * D].T

    mine = rows_at(core * HALF, HALF)
    send_a[...] = wg[rows_at((1 - core) * HALF, HALF), :].astype(BF)
    first = remote(send_a, recv_a, 0, mate)
    first.start()

    def give_back(k):
        def part(m, _):
            rows = rows_at(m * TE, TE)
            s = mm2(scatter_hot(snd_ref, k, m), g[k * E:(k + 1) * E, :])
            bsend[k - 1, rows, :] = wide_nt(s, w1).astype(BF)
            return 0
        lax.fori_loop(0, N // TE, part, 0)
        c = halo(bsend.at[k - 1], brecv.at[k - 1], 2 + k, (None, down, before, after)[k])
        c.start()
        return c

    homeward = [give_back(2)]
    first.wait()
    send_b[...] = (wg[mine, :] + recv_a[...].astype(F32)).astype(BF)
    copies = []
    for d, other in enumerate(plane, 1):
        copies.append(remote(send_b.at[rows_at(((spot + d) % XY) * PIECE, PIECE), :],
                             recv_b.at[spot], d, other))
        copies[-1].start()
    recv_b[spot] = send_b[rows_at(spot * PIECE, PIECE), :]
    homeward.append(give_back(3))
    homeward.append(give_back(1))
    for c in copies:
        c.wait()
    total = recv_b[0].astype(F32)
    for j in range(1, XY):
        total = total + recv_b[j].astype(F32)
    send_c[...] = total.astype(BF)
    copies = []
    for d, other in enumerate(line, 1):
        copies.append(remote(send_c, recv_c.at[z], XY + d, other))
        copies[-1].start()
    recv_c[z] = send_c[...]

    def own_part(m, _):
        rows = rows_at(m * TE, TE)
        s = mm2(scatter_hot(snd_ref, 0, m), g[0:E, :])
        r = mm2(oht[rows, :], g[...])
        hit_out[rows, :] += wide_nt(s, w1) + wide_nt(r, w2)
        return 0

    lax.fori_loop(0, N // TE, own_part, 0)
    for c in copies:
        c.wait()
    total = recv_c[0].astype(F32)
    for j in range(1, LZ):
        total = total + recv_c[j].astype(F32)
    send_d[...] = (total * (1.0 / 256.0)).astype(BF)
    here = rows_at(core * HALF + spot * PIECE, PIECE)
    copies = []
    for d, other in enumerate(plane, 1):
        copies.append(remote(send_d, fin.at[here, :], XY + LZ + d, other))
        copies[-1].start()
    fin[here, :] = send_d[...]

    def edges(n, _):
        rows = rows_at(n * TE, TE)
        ebuf[rows, :] = (ge[rows, :].astype(F32) + mm_nt(g[rows, :], w3)).astype(BF)
        return 0

    lax.fori_loop(0, KE // TE, edges, 0)
    store = pltpu.make_async_copy(ebuf, edge_out, sem_in.at[4])
    store.start()
    for c in copies:
        c.wait()
    last = remote(fin.at[mine, :], fin.at[mine, :], XY + LZ, mate)
    last.start()
    for c in homeward:
        c.wait()
    hit_out[...] += (brecv[0].astype(F32) + brecv[1].astype(F32)) + brecv[2].astype(F32)
    last.wait()
    store.wait()


def step_call(cnt, snd, rcv, hit, ef, gh, ge, wi, wo, ni, no):
    V = pl.BlockSpec(memory_space=pltpu.VMEM)
    H = pl.BlockSpec(memory_space=pl.ANY)
    sem = pltpu.SemaphoreType.DMA
    return pl.pallas_call(
        step_kernel,
        out_shape=(jax.ShapeDtypeStruct((N, D), F32), jax.ShapeDtypeStruct((KE, D), BF),
                   jax.ShapeDtypeStruct((8 * D, D), BF)),
        in_specs=[pl.BlockSpec(memory_space=pltpu.SMEM), V, V, H, H, H, H, V, V, V, V],
        out_specs=(V, H, V),
        scratch_shapes=[
            pltpu.VMEM((K, N, D), BF), pltpu.VMEM((KE, 3 * D), BF),
            pltpu.VMEM((N, D), BF), pltpu.VMEM((KE, D), BF),
            pltpu.VMEM((KE, D), jnp.int16), pltpu.VMEM((N, KE), BF), pltpu.VMEM((D, 4 * D), F32), pltpu.VMEM((KE, D), BF),
            pltpu.VMEM((KE, D), F32), pltpu.VMEM((KE, D), F32), pltpu.VMEM((KE, D), BF),
            pltpu.VMEM((KE, D), BF), pltpu.VMEM((KE, D), BF), pltpu.VMEM((N, 2 * D), BF),
            pltpu.VMEM((K, E // D, D), jnp.int32), pltpu.VMEM((K, E // D, D), jnp.int32),
            pltpu.VMEM((8 * D, D), F32),
            pltpu.VMEM((3, N, D), BF), pltpu.VMEM((3, N, D), BF),
            pltpu.VMEM((HALF, D), BF), pltpu.VMEM((HALF, D), BF), pltpu.VMEM((HALF, D), BF),
            pltpu.VMEM((XY, PIECE, D), BF), pltpu.VMEM((LZ, PIECE, D), BF),
            pltpu.VMEM((PIECE, D), BF), pltpu.VMEM((PIECE, D), BF),
            sem((5,)), sem((6,)), sem((6,)), sem((2 * XY + LZ,)), sem((2 * XY + LZ,)),
        ],
        compiler_params=pltpu.CompilerParams(
            vmem_limit_bytes=60 << 20, collective_id=0, has_side_effects=True),
        name="graph_step",
    )(cnt, snd, rcv, hit, ef, gh, ge, wi, wo, ni, no)


def finish_kernel(hits_in, edges_in, fin_in, hits, edges, g1, g2, g3, g4,
                  hbuf, ebuf, fbuf, wbuf, sem_i, sem_o):
    loads = [pltpu.make_async_copy(fin_in, fbuf, sem_i.at[0])]
    for k in range(K):
        part = pl.ds(k * E, E)
        loads.append(pltpu.make_async_copy(
            edges_in.at[part, :], ebuf.at[part, :], sem_i.at[k + 1]))
    loads.append(pltpu.make_async_copy(hits_in, hbuf, sem_i.at[5]))
    for c in loads:
        c.start()
    stores = []
    loads[0].wait()
    wbuf[...] = fbuf[...].astype(F32)
    first = 0
    for n, out in enumerate((g1, g2, g3, g4)):
        size = out.shape[0]
        stores.append(pltpu.make_async_copy(wbuf.at[pl.ds(first, size), :], out, sem_o.at[n]))
        stores[-1].start()
        first += size
    for k in range(K):
        part = pl.ds(k * E, E)
        loads[k + 1].wait()
        stores.append(pltpu.make_async_copy(ebuf.at[part, :], edges.at[part, :], sem_o.at[4 + k]))
        stores[-1].start()
    loads[5].wait()
    stores.append(pltpu.make_async_copy(hbuf, hits, sem_o.at[8]))
    stores[-1].start()
    for c in stores:
        c.wait()


def finish_call(hits, edges, fin):
    H = pl.BlockSpec(memory_space=pl.ANY)
    sem = pltpu.SemaphoreType.DMA
    shape = jax.ShapeDtypeStruct
    return pl.pallas_call(
        finish_kernel,
        out_shape=(shape((N, D), F32), shape((KE, D), BF), shape((3 * D, D), F32),
                   shape((D, D), F32), shape((2 * D, D), F32), shape((D, D), F32)),
        in_specs=[H, H, H],
        out_specs=(H,) * 6,
        scratch_shapes=[pltpu.VMEM((N, D), F32), pltpu.VMEM((KE, D), BF),
                        pltpu.VMEM((8 * D, D), BF), pltpu.VMEM((8 * D, D), F32),
                        sem((6,)), sem((9,))],
        compiler_params=pltpu.CompilerParams(vmem_limit_bytes=60 << 20),
        name="finish",
    )(hits, edges, fin)


def body(hit, ef, snd, rcv, cnt, gh, ge, wi, wo, ni, no):
    hits, edges, fin = step_call(
        cnt[0, 0], snd[0, 0], rcv[0, 0], hit[0, 0], ef[0, 0].reshape(KE, D),
        gh[0, 0], ge[0, 0].reshape(KE, D), wi, wo, ni, no)
    hits, edges, g1, g2, g3, g4 = finish_call(hits, edges, fin)
    return hits[None, None], edges.reshape(1, 1, K, E, D), g1, g2, g3, g4


def solution(mesh):
    two = P("layer", "phi", None, None)
    three = P("layer", "phi", None, None, None)
    return jax.shard_map(
        body, mesh=mesh,
        in_specs=(two, three, two, two, P("layer", "phi", None), two, three, P(), P(), P(), P()),
        out_specs=(two, three, P(), P(), P(), P()),
        check_vma=False,
    )
```

```python
import jax
import jax.numpy as jnp
from jax import lax
from jax.experimental import pallas as pl
from jax.experimental.pallas import tpu as pltpu
from jax.sharding import PartitionSpec as P

F32 = jnp.float32
BF = jnp.bfloat16
MESH = pl.DeviceIdType.MESH
N, E, D, K = 1024, 1024, 128, 4
KE = K * E
TE = 256
GT = 512
LZ, XY, HALF = 8, 16, 256
SEMS = 2 * XY + LZ
PIECE = HALF // XY


def mm(a, b):
    return jnp.dot(a, b, preferred_element_type=F32)


def mm2(a, b):
    return jnp.dot(a, jnp.concatenate([b, b], axis=1), preferred_element_type=F32)[:, 0:D]


def mm_nt(a, b):
    return lax.dot_general(a, b, (((1,), (1,)), ((), ())), preferred_element_type=F32)


def mm_tn(a, b):
    return lax.dot_general(a, b, (((0,), (0,)), ((), ())), preferred_element_type=F32)


def halves(x):
    hi = x.astype(BF)
    return hi, (x - hi.astype(F32)).astype(BF)


def wide_nt(x, w):
    hi, lo = halves(x)
    return mm_nt(hi, w) + mm_nt(lo, w)


def fold(x):
    return x[:, 0:D] + x[:, D:2 * D]


def gather_hot(col):
    lane = lax.broadcasted_iota(jnp.int16, (D, D), 1)
    return jnp.concatenate(
        [jnp.where(col == lane + jnp.int16(j * D), BF(1), BF(0)) for j in range(N // D)], axis=1)


def spread(idx_row):
    return jnp.broadcast_to(idx_row, (D, D)).T.astype(jnp.int16)


def tall_hot(cols):
    return jnp.concatenate([gather_hot(c) for c in cols], axis=0)


def scatter_hot(idx_ref, k, m):
    ids = idx_ref[k:k + 1, :].astype(jnp.int16)
    io = lax.broadcasted_iota(jnp.int16, (TE, E), 0) + (m * TE).astype(jnp.int16)
    return jnp.where(jnp.broadcast_to(ids, (TE, E)) == io, BF(1), BF(0))


def norm_parts(pre):
    mean = jnp.mean(pre, axis=-1, keepdims=True)
    c = pre - mean
    var = jnp.mean(c * c, axis=-1, keepdims=True)
    r = lax.rsqrt(var + 1e-5)
    u = c * r
    s = 0.5 + 0.5 * jnp.tanh(0.5 * u)
    h = u * s
    return u, h, r * (s + h * (1.0 - s))


def norm_back(w, u):
    return w - jnp.mean(w, axis=-1, keepdims=True) - u * jnp.mean(w * u, axis=-1, keepdims=True)


def rows_at(start, size):
    return pl.ds(pl.multiple_of(start, size), size)


def step_kernel(cnt_ref, snd_ref, rcv_ref, hit_any, ef_any, gh_any, ge_any,
                wi_ref, wo_ref, ni_ref, no_ref,
                hit_out, edge_out, fin,
                src, inp, gh, ge, rcol, oht, wt, ebuf, A, U, hid, g, mg, t3, si, ri, wg,
                bsend, brecv, send_a, recv_a, send_b, recv_b, recv_c, send_c, send_d,
                sem_in, sem_hs, sem_hr, sem_s, sem_r):
    layer = lax.axis_index("layer")
    phi = lax.axis_index("phi")
    core = layer % 2
    spot = ((phi // 32) * 2 + layer // 2) * 4 + phi % 4
    z = (phi // 4) % 8

    def at(c, s, zz):
        y = s // 4
        return ((y % 2) * 2 + c, (y // 2) * 32 + zz * 4 + s % 4)

    up = ((layer + 1) % 4, phi)
    down = ((layer + 3) % 4, phi)
    after = (layer, (phi + 1) % 64)
    before = (layer, (phi + 63) % 64)
    mate = at(1 - core, spot, z)
    plane = [at(core, (spot + d) % XY, z) for d in range(1, XY)]
    line = [at(core, spot, (z + d) % LZ) for d in range(1, LZ)]
    everyone = [up, down, after, before, mate] + plane + line
    barrier = pltpu.get_barrier_semaphore()
    for other in everyone:
        pl.semaphore_signal(barrier, inc=1, device_id=other, device_id_type=MESH)
    loads = [
        pltpu.make_async_copy(hit_any, src.at[0], sem_in.at[0]),
        pltpu.make_async_copy(ef_any, inp.at[:, 2 * D:3 * D], sem_in.at[1]),
        pltpu.make_async_copy(gh_any, gh, sem_in.at[2]),
        pltpu.make_async_copy(ge_any, ge, sem_in.at[3]),
    ]
    for c in loads:
        c.start()
    for k in range(K):
        for c in range(E // D):
            si[k, c:c + 1, :] = snd_ref[k:k + 1, c * D:(c + 1) * D]
            ri[k, c:c + 1, :] = rcv_ref[k:k + 1, c * D:(c + 1) * D]
    loads[0].wait()
    pl.semaphore_wait(barrier, len(everyone))

    def halo(s, d, n, to):
        return pltpu.make_async_remote_copy(
            src_ref=s, dst_ref=d, send_sem=sem_hs.at[n], recv_sem=sem_hr.at[n],
            device_id=to, device_id_type=MESH)

    def remote(s, d, n, to):
        return pltpu.make_async_remote_copy(
            src_ref=s, dst_ref=d, send_sem=sem_s.at[n], recv_sem=sem_r.at[n],
            device_id=to, device_id_type=MESH)

    outward = [halo(src.at[0], src.at[1], 0, up), halo(src.at[0], src.at[2], 1, after),
               halo(src.at[0], src.at[3], 2, before)]
    for c in outward:
        c.start()

    wi = wi_ref[...]
    w1, w2, w3 = wi[0:D, :], wi[D:2 * D, :], wi[2 * D:3 * D, :]
    wo = wo_ref[...]
    wn1, wn2 = ni_ref[0:D, :], ni_ref[D:2 * D, :]

    def receivers(k, _):
        for t in range(E // GT):
            cols = []
            for n in range(t * (GT // D), (t + 1) * (GT // D)):
                cols.append(spread(ri[k, n:n + 1, :]))
                rcol[rows_at(k * E + n * D, D), :] = cols[-1]
            inp[rows_at(k * E + t * GT, GT), D:2 * D] = mm2(tall_hot(cols), src[0]).astype(BF)
        return 0

    lax.fori_loop(0, K, receivers, 0)
    loads[1].wait()

    def senders(k, t):
        cols = [spread(si[k, n:n + 1, :]) for n in range(t * (GT // D), (t + 1) * (GT // D))]
        inp[rows_at(k * E + t * GT, GT), 0:D] = mm2(tall_hot(cols), src[k]).astype(BF)

    def hidden(k, t):
        rows = rows_at(k * E + t * GT, GT)
        u, h, d = norm_parts(mm2(inp[rows, :], wi))
        live = (lax.broadcasted_iota(jnp.int32, (GT, D), 0) + t * GT) < cnt_ref[k]
        U[rows, :] = u
        A[rows, :] = jnp.where(live, d, 0.0)
        hid[rows, :] = jnp.where(live, h, 0.0).astype(BF)

    tiles = [(k, t) for k in range(K) for t in range(E // GT)]
    for n, (k, t) in enumerate(tiles):
        if k and t == 0:
            outward[k - 1].wait()
        senders(k, t)
        if n:
            hidden(*tiles[n - 1])
    hidden(*tiles[-1])

    def collect(m, _):
        rows = rows_at(m * TE, TE)
        for k in range(K):
            oht[rows, k * E:(k + 1) * E] = scatter_hot(rcv_ref, k, m)
        hi, lo = halves(mm2(oht[rows, :], hid[...]))
        t3[rows, 0:D] = hi
        t3[rows, D:2 * D] = lo
        return 0

    lax.fori_loop(0, N // TE, collect, 0)
    loads[2].wait()
    incoming = (mm(t3[:, 0:D], wo) + mm(t3[:, D:2 * D], wo)).astype(BF)
    u, h, d = norm_parts(mm(src[0], wn1) + mm(incoming, wn2))
    ghv = gh[...]
    wg[6 * D:7 * D, :] = mm_tn(h.astype(BF), ghv)
    npg = norm_back(mm_nt(ghv, no_ref[...]) * d, u).astype(BF)
    wg[4 * D:5 * D, :] = mm_tn(src[0], npg)
    wg[5 * D:6 * D, :] = mm_tn(incoming, npg)
    wg[7 * D:8 * D, :] = jnp.zeros((D, D), F32)
    wt[...] = jnp.zeros((D, 4 * D), F32)
    hit_out[...] = ghv.astype(F32) + mm_nt(npg, wn1)
    hi, lo = halves(mm_nt(npg, wn2))
    t3[:, 0:D] = hi
    t3[:, D:2 * D] = lo
    loads[3].wait()

    def pull(k, t):
        base = k * E + t * GT
        rows = rows_at(base, GT)
        cols = [rcol[rows_at(base + n * D, D), :] for n in range(GT // D)]
        mg[rows, :] = (ge[rows, :].astype(F32)
                       + fold(mm(tall_hot(cols), t3[...]))).astype(BF)

    def chain(k, t):
        rows = rows_at(k * E + t * GT, GT)
        g[rows, :] = norm_back(mm_nt(mg[rows, :], wo) * A[rows, :], U[rows, :]).astype(BF)

    def weights(k):
        rows = rows_at(k * E, E)
        wt[:, 0:3 * D] += mm_tn(g[rows, :], inp[rows, :])
        wt[:, 3 * D:4 * D] += mm_tn(mg[rows, :], hid[rows, :])

    def meet_mate(q):
        send_a[q] = wg[rows_at(q * 2 * HALF + (1 - core) * HALF, HALF), :].astype(BF)
        c = remote(send_a.at[q], recv_a.at[q], q * SEMS, mate)
        c.start()
        return c

    def spread_plane(q, c):
        c.wait()
        own = wg[rows_at(q * 2 * HALF + core * HALF, HALF), :]
        send_b[q] = (own + recv_a[q].astype(F32)).astype(BF)
        copies = []
        for d, other in enumerate(plane, 1):
            piece = rows_at(((spot + d) % XY) * PIECE, PIECE)
            copies.append(remote(send_b.at[q, piece, :], recv_b.at[q, spot], q * SEMS + d, other))
            copies[-1].start()
        recv_b[q, spot] = send_b[q, rows_at(spot * PIECE, PIECE), :]
        return copies

    def spread_line(q, copies):
        for c in copies:
            c.wait()
        total = recv_b[q, 0].astype(F32)
        for j in range(1, XY):
            total = total + recv_b[q, j].astype(F32)
        send_c[q] = total.astype(BF)
        copies = []
        for d, other in enumerate(line, 1):
            copies.append(remote(send_c.at[q], recv_c.at[q, z], q * SEMS + XY + d, other))
            copies[-1].start()
        recv_c[q, z] = send_c[q]
        return copies

    def gather_plane(q, copies):
        for c in copies:
            c.wait()
        total = recv_c[q, 0].astype(F32)
        for j in range(1, LZ):
            total = total + recv_c[q, j].astype(F32)
        send_d[q] = (total * (1.0 / 256.0)).astype(BF)
        here = rows_at(q * 2 * HALF + core * HALF + spot * PIECE, PIECE)
        copies = []
        for d, other in enumerate(plane, 1):
            copies.append(remote(send_d.at[q], fin.at[here, :], q * SEMS + XY + LZ + d, other))
            copies[-1].start()
        fin[here, :] = send_d[q]
        return copies

    def gather_mate(q, copies):
        for c in copies:
            c.wait()
        mine = rows_at(q * 2 * HALF + core * HALF, HALF)
        c = remote(fin.at[mine, :], fin.at[mine, :], q * SEMS + XY + LZ, mate)
        c.start()
        return c

    early = meet_mate(1)
    for n, (k, t) in enumerate(tiles):
        pull(k, t)
        if n:
            chain(*tiles[n - 1])
        if k and t == 1:
            weights(k - 1)
        if n == 3:
            early = spread_plane(1, early)
    chain(*tiles[-1])
    weights(K - 1)
    for j in range(4):
        wg[j * D:(j + 1) * D, :] = wt[:, j * D:(j + 1) * D].T

    late = meet_mate(0)

    def give_back(k):
        def part(m, _):
            rows = rows_at(m * TE, TE)
            s = mm2(scatter_hot(snd_ref, k, m), g[k * E:(k + 1) * E, :])
            bsend[k - 1, rows, :] = wide_nt(s, w1).astype(BF)
            return 0
        lax.fori_loop(0, N // TE, part, 0)
        return halo(bsend.at[k - 1], brecv.at[k - 1], 2 + k, (None, down, before, after)[k])

    early = spread_line(1, early)
    homeward = [give_back(2)]
    late = spread_plane(0, late)
    homeward[0].start()
    for k in (3, 1):
        homeward.append(give_back(k))
        homeward[-1].start()
    early = gather_plane(1, early)
    late = spread_line(0, late)

    def own_part(m, _):
        rows = rows_at(m * TE, TE)
        s = mm2(scatter_hot(snd_ref, 0, m), g[0:E, :])
        r = mm2(oht[rows, :], g[...])
        hit_out[rows, :] += wide_nt(s, w1) + wide_nt(r, w2)
        return 0

    lax.fori_loop(0, N // TE, own_part, 0)
    late = gather_plane(0, late)

    def edges(n, _):
        rows = rows_at(n * TE, TE)
        ebuf[rows, :] = (ge[rows, :].astype(F32) + mm_nt(g[rows, :], w3)).astype(BF)
        return 0

    lax.fori_loop(0, KE // TE, edges, 0)
    store = pltpu.make_async_copy(ebuf, edge_out, sem_in.at[4])
    store.start()
    early = gather_mate(1, early)
    late = gather_mate(0, late)
    for c in homeward:
        c.wait()
    hit_out[...] += (brecv[0].astype(F32) + brecv[1].astype(F32)) + brecv[2].astype(F32)
    early.wait()
    late.wait()
    store.wait()


def step_call(cnt, snd, rcv, hit, ef, gh, ge, wi, wo, ni, no):
    V = pl.BlockSpec(memory_space=pltpu.VMEM)
    H = pl.BlockSpec(memory_space=pl.ANY)
    sem = pltpu.SemaphoreType.DMA
    return pl.pallas_call(
        step_kernel,
        out_shape=(jax.ShapeDtypeStruct((N, D), F32), jax.ShapeDtypeStruct((KE, D), BF),
                   jax.ShapeDtypeStruct((8 * D, D), BF)),
        in_specs=[pl.BlockSpec(memory_space=pltpu.SMEM), V, V, H, H, H, H, V, V, V, V],
        out_specs=(V, H, V),
        scratch_shapes=[
            pltpu.VMEM((K, N, D), BF), pltpu.VMEM((KE, 3 * D), BF),
            pltpu.VMEM((N, D), BF), pltpu.VMEM((KE, D), BF),
            pltpu.VMEM((KE, D), jnp.int16), pltpu.VMEM((N, KE), BF), pltpu.VMEM((D, 4 * D), F32), pltpu.VMEM((KE, D), BF),
            pltpu.VMEM((KE, D), F32), pltpu.VMEM((KE, D), F32), pltpu.VMEM((KE, D), BF),
            pltpu.VMEM((KE, D), BF), pltpu.VMEM((KE, D), BF), pltpu.VMEM((N, 2 * D), BF),
            pltpu.VMEM((K, E // D, D), jnp.int32), pltpu.VMEM((K, E // D, D), jnp.int32),
            pltpu.VMEM((8 * D, D), F32),
            pltpu.VMEM((3, N, D), BF), pltpu.VMEM((3, N, D), BF),
            pltpu.VMEM((2, HALF, D), BF), pltpu.VMEM((2, HALF, D), BF), pltpu.VMEM((2, HALF, D), BF),
            pltpu.VMEM((2, XY, PIECE, D), BF), pltpu.VMEM((2, LZ, PIECE, D), BF),
            pltpu.VMEM((2, PIECE, D), BF), pltpu.VMEM((2, PIECE, D), BF),
            sem((5,)), sem((6,)), sem((6,)), sem((2 * SEMS,)), sem((2 * SEMS,)),
        ],
        compiler_params=pltpu.CompilerParams(
            vmem_limit_bytes=60 << 20, collective_id=0, has_side_effects=True),
        name="graph_step",
    )(cnt, snd, rcv, hit, ef, gh, ge, wi, wo, ni, no)


def finish_kernel(hits_in, edges_in, fin_in, hits, edges, g1, g2, g3, g4,
                  hbuf, ebuf, fbuf, wbuf, sem_i, sem_o):
    loads = [pltpu.make_async_copy(fin_in, fbuf, sem_i.at[0])]
    for k in range(K):
        part = pl.ds(k * E, E)
        loads.append(pltpu.make_async_copy(
            edges_in.at[part, :], ebuf.at[part, :], sem_i.at[k + 1]))
    loads.append(pltpu.make_async_copy(hits_in, hbuf, sem_i.at[5]))
    for c in loads:
        c.start()
    stores = []
    loads[0].wait()
    wbuf[...] = fbuf[...].astype(F32)
    first = 0
    for n, out in enumerate((g1, g2, g3, g4)):
        size = out.shape[0]
        stores.append(pltpu.make_async_copy(wbuf.at[pl.ds(first, size), :], out, sem_o.at[n]))
        stores[-1].start()
        first += size
    for k in range(K):
        part = pl.ds(k * E, E)
        loads[k + 1].wait()
        stores.append(pltpu.make_async_copy(ebuf.at[part, :], edges.at[part, :], sem_o.at[4 + k]))
        stores[-1].start()
    loads[5].wait()
    stores.append(pltpu.make_async_copy(hbuf, hits, sem_o.at[8]))
    stores[-1].start()
    for c in stores:
        c.wait()


def finish_call(hits, edges, fin):
    H = pl.BlockSpec(memory_space=pl.ANY)
    sem = pltpu.SemaphoreType.DMA
    shape = jax.ShapeDtypeStruct
    return pl.pallas_call(
        finish_kernel,
        out_shape=(shape((N, D), F32), shape((KE, D), BF), shape((3 * D, D), F32),
                   shape((D, D), F32), shape((2 * D, D), F32), shape((D, D), F32)),
        in_specs=[H, H, H],
        out_specs=(H,) * 6,
        scratch_shapes=[pltpu.VMEM((N, D), F32), pltpu.VMEM((KE, D), BF),
                        pltpu.VMEM((8 * D, D), BF), pltpu.VMEM((8 * D, D), F32),
                        sem((6,)), sem((9,))],
        compiler_params=pltpu.CompilerParams(vmem_limit_bytes=60 << 20),
        name="finish",
    )(hits, edges, fin)


def body(hit, ef, snd, rcv, cnt, gh, ge, wi, wo, ni, no):
    hits, edges, fin = step_call(
        cnt[0, 0], snd[0, 0], rcv[0, 0], hit[0, 0], ef[0, 0].reshape(KE, D),
        gh[0, 0], ge[0, 0].reshape(KE, D), wi, wo, ni, no)
    hits, edges, g1, g2, g3, g4 = finish_call(hits, edges, fin)
    return hits[None, None], edges.reshape(1, 1, K, E, D), g1, g2, g3, g4


def solution(mesh):
    two = P("layer", "phi", None, None)
    three = P("layer", "phi", None, None, None)
    return jax.shard_map(
        body, mesh=mesh,
        in_specs=(two, three, two, two, P("layer", "phi", None), two, three, P(), P(), P(), P()),
        out_specs=(two, three, P(), P(), P(), P()),
        check_vma=False,
    )
```

```python
import jax
import jax.numpy as jnp
from jax import lax
from jax.experimental import pallas as pl
from jax.experimental.pallas import tpu as pltpu
from jax.sharding import PartitionSpec as P

F32 = jnp.float32
BF = jnp.bfloat16
MESH = pl.DeviceIdType.MESH
N, E, D, K = 1024, 1024, 128, 4
KE = K * E
TE = 256
GT = 512
ST = 512
LZ, XY, HALF = 8, 16, 256
SEMS = 2 * XY + LZ
PIECE = HALF // XY


def mm(a, b):
    return jnp.dot(a, b, preferred_element_type=F32)


def mm2(a, b):
    return jnp.dot(a, jnp.concatenate([b, b], axis=1), preferred_element_type=F32)[:, 0:D]


def mm_nt(a, b):
    return lax.dot_general(a, b, (((1,), (1,)), ((), ())), preferred_element_type=F32)


def mm_tn(a, b):
    return lax.dot_general(a, b, (((0,), (0,)), ((), ())), preferred_element_type=F32)


def halves(x):
    hi = x.astype(BF)
    return hi, (x - hi.astype(F32)).astype(BF)


def wide_nt(x, w):
    both = jnp.concatenate(halves(x), axis=1)
    row = jnp.concatenate([w, w], axis=1)
    return mm_nt(both, jnp.concatenate([row, row], axis=0))[:, 0:D]


def fold(x):
    return x[:, 0:D] + x[:, D:2 * D]


def gather_hot(col):
    lane = lax.broadcasted_iota(jnp.int16, (D, D), 1)
    return jnp.concatenate(
        [jnp.where(col == lane + jnp.int16(j * D), BF(1), BF(0)) for j in range(N // D)], axis=1)


def spread(idx_row):
    return jnp.broadcast_to(idx_row, (D, D)).T.astype(jnp.int16)


def tall_hot(cols):
    return jnp.concatenate([gather_hot(c) for c in cols], axis=0)


def scatter_hot(idx_ref, k, m):
    ids = idx_ref[k:k + 1, :].astype(jnp.int16)
    io = lax.broadcasted_iota(jnp.int16, (ST, E), 0) + jnp.int16(m * ST)
    return jnp.where(jnp.broadcast_to(ids, (ST, E)) == io, BF(1), BF(0))


def receiver_hot(idx_ref, m):
    return jnp.concatenate([scatter_hot(idx_ref, k, m) for k in range(K)], axis=1)


def norm_parts(pre):
    mean = jnp.mean(pre, axis=-1, keepdims=True)
    c = pre - mean
    var = jnp.mean(c * c, axis=-1, keepdims=True)
    r = lax.rsqrt(var + 1e-5)
    u = c * r
    s = 0.5 + 0.5 * jnp.tanh(0.5 * u)
    h = u * s
    return u, h, r * (s + h * (1.0 - s))


def norm_back(w, u):
    return w - jnp.mean(w, axis=-1, keepdims=True) - u * jnp.mean(w * u, axis=-1, keepdims=True)


def rows_at(start, size):
    return pl.ds(pl.multiple_of(start, size), size)


def step_kernel(cnt_ref, snd_ref, rcv_ref, hit_any, ef_any, gh_any, ge_any,
                wi_ref, wo_ref, ni_ref, no_ref,
                hit_out, edge_out, fin,
                src, inp, gh, ge, rcol, wt, ebuf, A, U, hid, g, mg, t3, si, ri, wg,
                bsend, brecv, send_a, recv_a, send_b, recv_b, recv_c, send_c, send_d,
                sem_in, sem_hs, sem_hr, sem_s, sem_r):
    layer = lax.axis_index("layer")
    phi = lax.axis_index("phi")
    core = layer % 2
    spot = ((phi // 32) * 2 + layer // 2) * 4 + phi % 4
    z = (phi // 4) % 8

    def at(c, s, zz):
        y = s // 4
        return ((y % 2) * 2 + c, (y // 2) * 32 + zz * 4 + s % 4)

    up = ((layer + 1) % 4, phi)
    down = ((layer + 3) % 4, phi)
    after = (layer, (phi + 1) % 64)
    before = (layer, (phi + 63) % 64)
    mate = at(1 - core, spot, z)
    plane = [at(core, (spot + d) % XY, z) for d in range(1, XY)]
    line = [at(core, spot, (z + d) % LZ) for d in range(1, LZ)]
    everyone = [up, down, after, before, mate] + plane + line
    barrier = pltpu.get_barrier_semaphore()
    for other in everyone:
        pl.semaphore_signal(barrier, inc=1, device_id=other, device_id_type=MESH)
    loads = [
        pltpu.make_async_copy(hit_any, src.at[0], sem_in.at[0]),
        pltpu.make_async_copy(ef_any, inp.at[:, 2 * D:3 * D], sem_in.at[1]),
        pltpu.make_async_copy(gh_any, gh, sem_in.at[2]),
        pltpu.make_async_copy(ge_any, ge, sem_in.at[3]),
    ]
    for c in loads:
        c.start()
    for k in range(K):
        for c in range(E // D):
            si[k, c:c + 1, :] = snd_ref[k:k + 1, c * D:(c + 1) * D]
            ri[k, c:c + 1, :] = rcv_ref[k:k + 1, c * D:(c + 1) * D]
    loads[0].wait()
    pl.semaphore_wait(barrier, len(everyone))

    def halo(s, d, n, to):
        return pltpu.make_async_remote_copy(
            src_ref=s, dst_ref=d, send_sem=sem_hs.at[n], recv_sem=sem_hr.at[n],
            device_id=to, device_id_type=MESH)

    def remote(s, d, n, to):
        return pltpu.make_async_remote_copy(
            src_ref=s, dst_ref=d, send_sem=sem_s.at[n], recv_sem=sem_r.at[n],
            device_id=to, device_id_type=MESH)

    outward = [halo(src.at[0], src.at[1], 0, up), halo(src.at[0], src.at[2], 1, after),
               halo(src.at[0], src.at[3], 2, before)]
    for c in outward:
        c.start()

    wi = wi_ref[...]
    w1, w2, w3 = wi[0:D, :], wi[D:2 * D, :], wi[2 * D:3 * D, :]
    wo = wo_ref[...]
    wn1, wn2 = ni_ref[0:D, :], ni_ref[D:2 * D, :]

    def receivers(k, _):
        for t in range(E // GT):
            cols = []
            for n in range(t * (GT // D), (t + 1) * (GT // D)):
                cols.append(spread(ri[k, n:n + 1, :]))
                rcol[rows_at(k * E + n * D, D), :] = cols[-1]
            inp[rows_at(k * E + t * GT, GT), D:2 * D] = mm2(tall_hot(cols), src[0]).astype(BF)
        return 0

    lax.fori_loop(0, K, receivers, 0)
    loads[1].wait()

    def senders(k, t):
        cols = [spread(si[k, n:n + 1, :]) for n in range(t * (GT // D), (t + 1) * (GT // D))]
        inp[rows_at(k * E + t * GT, GT), 0:D] = mm2(tall_hot(cols), src[k]).astype(BF)

    def hidden(k, t):
        rows = rows_at(k * E + t * GT, GT)
        u, h, d = norm_parts(mm2(inp[rows, :], wi))
        live = (lax.broadcasted_iota(jnp.int32, (GT, D), 0) + t * GT) < cnt_ref[k]
        U[rows, :] = u
        A[rows, :] = jnp.where(live, d, 0.0)
        hid[rows, :] = jnp.where(live, h, 0.0).astype(BF)

    tiles = [(k, t) for k in range(K) for t in range(E // GT)]
    for n, (k, t) in enumerate(tiles):
        if k and t == 0:
            outward[k - 1].wait()
        senders(k, t)
        if n:
            hidden(*tiles[n - 1])
    hidden(*tiles[-1])

    for m in range(N // ST):
        rows = rows_at(m * ST, ST)
        hi, lo = halves(mm2(receiver_hot(rcv_ref, m), hid[...]))
        t3[rows, 0:D] = hi
        t3[rows, D:2 * D] = lo
    loads[2].wait()
    incoming = (mm(t3[:, 0:D], wo) + mm(t3[:, D:2 * D], wo)).astype(BF)
    u, h, d = norm_parts(mm(src[0], wn1) + mm(incoming, wn2))
    ghv = gh[...]
    wg[6 * D:7 * D, :] = mm_tn(h.astype(BF), ghv)
    npg = norm_back(mm_nt(ghv, no_ref[...]) * d, u).astype(BF)
    wg[4 * D:5 * D, :] = mm_tn(src[0], npg)
    wg[5 * D:6 * D, :] = mm_tn(incoming, npg)
    wg[7 * D:8 * D, :] = jnp.zeros((D, D), F32)
    wt[...] = jnp.zeros((D, 4 * D), F32)
    hit_out[...] = ghv.astype(F32) + mm_nt(npg, wn1)
    hi, lo = halves(mm_nt(npg, wn2))
    t3[:, 0:D] = hi
    t3[:, D:2 * D] = lo
    loads[3].wait()

    def pull(k, t):
        base = k * E + t * GT
        rows = rows_at(base, GT)
        cols = [rcol[rows_at(base + n * D, D), :] for n in range(GT // D)]
        mg[rows, :] = (ge[rows, :].astype(F32)
                       + fold(mm(tall_hot(cols), t3[...]))).astype(BF)

    def chain(k, t):
        rows = rows_at(k * E + t * GT, GT)
        g[rows, :] = norm_back(mm_nt(mg[rows, :], wo) * A[rows, :], U[rows, :]).astype(BF)

    def weights(k):
        rows = rows_at(k * E, E)
        wt[:, 0:3 * D] += mm_tn(g[rows, :], inp[rows, :])
        wt[:, 3 * D:4 * D] += mm_tn(mg[rows, :], hid[rows, :])

    def meet_mate(q):
        send_a[q] = wg[rows_at(q * 2 * HALF + (1 - core) * HALF, HALF), :].astype(BF)
        c = remote(send_a.at[q], recv_a.at[q], q * SEMS, mate)
        c.start()
        return c

    def spread_plane(q, c):
        c.wait()
        own = wg[rows_at(q * 2 * HALF + core * HALF, HALF), :]
        send_b[q] = (own + recv_a[q].astype(F32)).astype(BF)
        copies = []
        for d, other in enumerate(plane, 1):
            piece = rows_at(((spot + d) % XY) * PIECE, PIECE)
            copies.append(remote(send_b.at[q, piece, :], recv_b.at[q, spot], q * SEMS + d, other))
            copies[-1].start()
        recv_b[q, spot] = send_b[q, rows_at(spot * PIECE, PIECE), :]
        return copies

    def spread_line(q, copies):
        for c in copies:
            c.wait()
        total = recv_b[q, 0].astype(F32)
        for j in range(1, XY):
            total = total + recv_b[q, j].astype(F32)
        send_c[q] = total.astype(BF)
        copies = []
        for d, other in enumerate(line, 1):
            copies.append(remote(send_c.at[q], recv_c.at[q, z], q * SEMS + XY + d, other))
            copies[-1].start()
        recv_c[q, z] = send_c[q]
        return copies

    def gather_plane(q, copies):
        for c in copies:
            c.wait()
        total = recv_c[q, 0].astype(F32)
        for j in range(1, LZ):
            total = total + recv_c[q, j].astype(F32)
        send_d[q] = (total * (1.0 / 256.0)).astype(BF)
        here = rows_at(q * 2 * HALF + core * HALF + spot * PIECE, PIECE)
        copies = []
        for d, other in enumerate(plane, 1):
            copies.append(remote(send_d.at[q], fin.at[here, :], q * SEMS + XY + LZ + d, other))
            copies[-1].start()
        fin[here, :] = send_d[q]
        return copies

    def gather_mate(q, copies):
        for c in copies:
            c.wait()
        mine = rows_at(q * 2 * HALF + core * HALF, HALF)
        c = remote(fin.at[mine, :], fin.at[mine, :], q * SEMS + XY + LZ, mate)
        c.start()
        return c

    early = meet_mate(1)
    for n, (k, t) in enumerate(tiles):
        pull(k, t)
        if n:
            chain(*tiles[n - 1])
        if k and t == 1:
            weights(k - 1)
        if n == 3:
            early = spread_plane(1, early)
    chain(*tiles[-1])
    weights(K - 1)
    for j in range(4):
        wg[j * D:(j + 1) * D, :] = wt[:, j * D:(j + 1) * D].T

    late = meet_mate(0)

    def give_back(k):
        for m in range(N // ST):
            rows = rows_at(m * ST, ST)
            s = mm2(scatter_hot(snd_ref, k, m), g[k * E:(k + 1) * E, :])
            bsend[k - 1, rows, :] = wide_nt(s, w1).astype(BF)
        return halo(bsend.at[k - 1], brecv.at[k - 1], 2 + k, (None, down, before, after)[k])

    early = spread_line(1, early)
    homeward = [give_back(2)]
    late = spread_plane(0, late)
    homeward[0].start()
    for k in (3, 1):
        homeward.append(give_back(k))
        homeward[-1].start()
    early = gather_plane(1, early)
    late = spread_line(0, late)

    for m in range(N // ST):
        rows = rows_at(m * ST, ST)
        hit_out[rows, :] += wide_nt(mm2(scatter_hot(snd_ref, 0, m), g[0:E, :]), w1)
    for m in range(N // ST):
        rows = rows_at(m * ST, ST)
        hi, lo = halves(mm2(receiver_hot(rcv_ref, m), g[...]))
        t3[rows, 0:D] = hi
        t3[rows, D:2 * D] = lo
    row = jnp.concatenate([w2, w2], axis=1)
    for m in range(N // ST):
        rows = rows_at(m * ST, ST)
        hit_out[rows, :] += mm_nt(t3[rows, :], jnp.concatenate([row, row], axis=0))[:, 0:D]
    late = gather_plane(0, late)

    for n in range(KE // GT):
        rows = rows_at(n * GT, GT)
        ebuf[rows, :] = (ge[rows, :].astype(F32) + mm_nt(g[rows, :], w3)).astype(BF)
    store = pltpu.make_async_copy(ebuf, edge_out, sem_in.at[4])
    store.start()
    early = gather_mate(1, early)
    late = gather_mate(0, late)
    for c in homeward:
        c.wait()
    hit_out[...] += (brecv[0].astype(F32) + brecv[1].astype(F32)) + brecv[2].astype(F32)
    early.wait()
    late.wait()
    store.wait()


def step_call(cnt, snd, rcv, hit, ef, gh, ge, wi, wo, ni, no):
    V = pl.BlockSpec(memory_space=pltpu.VMEM)
    H = pl.BlockSpec(memory_space=pl.ANY)
    sem = pltpu.SemaphoreType.DMA
    return pl.pallas_call(
        step_kernel,
        out_shape=(jax.ShapeDtypeStruct((N, D), F32), jax.ShapeDtypeStruct((KE, D), BF),
                   jax.ShapeDtypeStruct((8 * D, D), BF)),
        in_specs=[pl.BlockSpec(memory_space=pltpu.SMEM), V, V, H, H, H, H, V, V, V, V],
        out_specs=(V, H, V),
        scratch_shapes=[
            pltpu.VMEM((K, N, D), BF), pltpu.VMEM((KE, 3 * D), BF),
            pltpu.VMEM((N, D), BF), pltpu.VMEM((KE, D), BF),
            pltpu.VMEM((KE, D), jnp.int16), pltpu.VMEM((D, 4 * D), F32), pltpu.VMEM((KE, D), BF),
            pltpu.VMEM((KE, D), F32), pltpu.VMEM((KE, D), F32), pltpu.VMEM((KE, D), BF),
            pltpu.VMEM((KE, D), BF), pltpu.VMEM((KE, D), BF), pltpu.VMEM((N, 2 * D), BF),
            pltpu.VMEM((K, E // D, D), jnp.int32), pltpu.VMEM((K, E // D, D), jnp.int32),
            pltpu.VMEM((8 * D, D), F32),
            pltpu.VMEM((3, N, D), BF), pltpu.VMEM((3, N, D), BF),
            pltpu.VMEM((2, HALF, D), BF), pltpu.VMEM((2, HALF, D), BF), pltpu.VMEM((2, HALF, D), BF),
            pltpu.VMEM((2, XY, PIECE, D), BF), pltpu.VMEM((2, LZ, PIECE, D), BF),
            pltpu.VMEM((2, PIECE, D), BF), pltpu.VMEM((2, PIECE, D), BF),
            sem((5,)), sem((6,)), sem((6,)), sem((2 * SEMS,)), sem((2 * SEMS,)),
        ],
        compiler_params=pltpu.CompilerParams(
            vmem_limit_bytes=60 << 20, collective_id=0, has_side_effects=True),
        name="graph_step",
    )(cnt, snd, rcv, hit, ef, gh, ge, wi, wo, ni, no)


def finish_kernel(hits_in, edges_in, fin_in, hits, edges, g1, g2, g3, g4,
                  hbuf, ebuf, fbuf, wbuf, sem_i, sem_o):
    loads = [pltpu.make_async_copy(fin_in, fbuf, sem_i.at[0])]
    for k in range(K):
        part = pl.ds(k * E, E)
        loads.append(pltpu.make_async_copy(
            edges_in.at[part, :], ebuf.at[part, :], sem_i.at[k + 1]))
    loads.append(pltpu.make_async_copy(hits_in, hbuf, sem_i.at[5]))
    for c in loads:
        c.start()
    stores = []
    loads[0].wait()
    wbuf[...] = fbuf[...].astype(F32)
    first = 0
    for n, out in enumerate((g1, g2, g3, g4)):
        size = out.shape[0]
        stores.append(pltpu.make_async_copy(wbuf.at[pl.ds(first, size), :], out, sem_o.at[n]))
        stores[-1].start()
        first += size
    for k in range(K):
        part = pl.ds(k * E, E)
        loads[k + 1].wait()
        stores.append(pltpu.make_async_copy(ebuf.at[part, :], edges.at[part, :], sem_o.at[4 + k]))
        stores[-1].start()
    loads[5].wait()
    stores.append(pltpu.make_async_copy(hbuf, hits, sem_o.at[8]))
    stores[-1].start()
    for c in stores:
        c.wait()


def finish_call(hits, edges, fin):
    H = pl.BlockSpec(memory_space=pl.ANY)
    sem = pltpu.SemaphoreType.DMA
    shape = jax.ShapeDtypeStruct
    return pl.pallas_call(
        finish_kernel,
        out_shape=(shape((N, D), F32), shape((KE, D), BF), shape((3 * D, D), F32),
                   shape((D, D), F32), shape((2 * D, D), F32), shape((D, D), F32)),
        in_specs=[H, H, H],
        out_specs=(H,) * 6,
        scratch_shapes=[pltpu.VMEM((N, D), F32), pltpu.VMEM((KE, D), BF),
                        pltpu.VMEM((8 * D, D), BF), pltpu.VMEM((8 * D, D), F32),
                        sem((6,)), sem((9,))],
        compiler_params=pltpu.CompilerParams(vmem_limit_bytes=60 << 20),
        name="finish",
    )(hits, edges, fin)


def body(hit, ef, snd, rcv, cnt, gh, ge, wi, wo, ni, no):
    hits, edges, fin = step_call(
        cnt[0, 0], snd[0, 0], rcv[0, 0], hit[0, 0], ef[0, 0].reshape(KE, D),
        gh[0, 0], ge[0, 0].reshape(KE, D), wi, wo, ni, no)
    hits, edges, g1, g2, g3, g4 = finish_call(hits, edges, fin)
    return hits[None, None], edges.reshape(1, 1, K, E, D), g1, g2, g3, g4


def solution(mesh):
    two = P("layer", "phi", None, None)
    three = P("layer", "phi", None, None, None)
    return jax.shard_map(
        body, mesh=mesh,
        in_specs=(two, three, two, two, P("layer", "phi", None), two, three, P(), P(), P(), P()),
        out_specs=(two, three, P(), P(), P(), P()),
        check_vma=False,
    )
```

```python
import jax
import jax.numpy as jnp
from jax import lax
from jax.experimental import pallas as pl
from jax.experimental.pallas import tpu as pltpu
from jax.sharding import PartitionSpec as P

F32 = jnp.float32
BF = jnp.bfloat16
MESH = pl.DeviceIdType.MESH
N, E, D, K = 1024, 1024, 128, 4
KE = K * E
TE = 256
GT = 512
ST = 512
LZ, XY, HALF = 8, 16, 256
SEMS = 2 * XY + LZ
PIECE = HALF // XY


def mm(a, b):
    return jnp.dot(a, b, preferred_element_type=F32)


def mm2(a, b):
    return jnp.dot(a, jnp.concatenate([b, b], axis=1), preferred_element_type=F32)[:, 0:D]


def mm_nt(a, b):
    return lax.dot_general(a, b, (((1,), (1,)), ((), ())), preferred_element_type=F32)


def mm_tn(a, b):
    return lax.dot_general(a, b, (((0,), (0,)), ((), ())), preferred_element_type=F32)


def halves(x):
    hi = x.astype(BF)
    return hi, (x - hi.astype(F32)).astype(BF)


def wide_nt(x, w):
    both = jnp.concatenate(halves(x), axis=1)
    row = jnp.concatenate([w, w], axis=1)
    return mm_nt(both, jnp.concatenate([row, row], axis=0))[:, 0:D]


def fold(x):
    return x[:, 0:D] + x[:, D:2 * D]


def gather_hot(col):
    lane = lax.broadcasted_iota(jnp.int16, (D, D), 1)
    return jnp.concatenate(
        [jnp.where(col == lane + jnp.int16(j * D), BF(1), BF(0)) for j in range(N // D)], axis=1)


def spread(idx_row):
    return jnp.broadcast_to(idx_row, (D, D)).T.astype(jnp.int16)


def tall_hot(cols):
    return jnp.concatenate([gather_hot(c) for c in cols], axis=0)


def scatter_hot(idx_ref, k, m):
    ids = idx_ref[k:k + 1, :].astype(jnp.int16)
    io = lax.broadcasted_iota(jnp.int16, (ST, E), 0) + jnp.int16(m * ST)
    return jnp.where(jnp.broadcast_to(ids, (ST, E)) == io, BF(1), BF(0))


def receiver_hot(idx_ref, m):
    return jnp.concatenate([scatter_hot(idx_ref, k, m) for k in range(K)], axis=1)


def norm_parts(pre):
    mean = jnp.mean(pre, axis=-1, keepdims=True)
    c = pre - mean
    var = jnp.mean(c * c, axis=-1, keepdims=True)
    r = lax.rsqrt(var + 1e-5)
    u = c * r
    s = 0.5 + 0.5 * jnp.tanh(0.5 * u)
    h = u * s
    return u, h, r * (s + h * (1.0 - s))


def norm_back(w, u):
    return w - jnp.mean(w, axis=-1, keepdims=True) - u * jnp.mean(w * u, axis=-1, keepdims=True)


def rows_at(start, size):
    return pl.ds(pl.multiple_of(start, size), size)


def step_kernel(cnt_ref, snd_ref, rcv_ref, hit_any, ef_any, gh_any, ge_any,
                wi_ref, wo_ref, ni_ref, no_ref,
                hit_out, edge_out, fin,
                src, inp, gh, ge, rcol, wt, ebuf, A, U, hid, g, mg, t3, si, ri, wg,
                bsend, brecv, send_a, recv_a, send_b, recv_b, recv_c, send_c, send_d,
                sem_in, sem_hs, sem_hr, sem_s, sem_r):
    layer = lax.axis_index("layer")
    phi = lax.axis_index("phi")
    core = layer % 2
    spot = ((phi // 32) * 2 + layer // 2) * 4 + phi % 4
    z = (phi // 4) % 8

    def at(c, s, zz):
        y = s // 4
        return ((y % 2) * 2 + c, (y // 2) * 32 + zz * 4 + s % 4)

    up = ((layer + 1) % 4, phi)
    down = ((layer + 3) % 4, phi)
    after = (layer, (phi + 1) % 64)
    before = (layer, (phi + 63) % 64)
    mate = at(1 - core, spot, z)
    plane = [at(core, (spot + d) % XY, z) for d in range(1, XY)]
    line = [at(core, spot, (z + d) % LZ) for d in range(1, LZ)]
    everyone = [up, down, after, before, mate] + plane + line
    barrier = pltpu.get_barrier_semaphore()
    for other in everyone:
        pl.semaphore_signal(barrier, inc=1, device_id=other, device_id_type=MESH)
    loads = [
        pltpu.make_async_copy(hit_any, src.at[0], sem_in.at[0]),
        pltpu.make_async_copy(ef_any, inp.at[:, 2 * D:3 * D], sem_in.at[1]),
        pltpu.make_async_copy(gh_any, gh, sem_in.at[2]),
        pltpu.make_async_copy(ge_any, ge, sem_in.at[3]),
    ]
    for c in loads:
        c.start()
    for k in range(K):
        for c in range(E // D):
            si[k, c:c + 1, :] = snd_ref[k:k + 1, c * D:(c + 1) * D]
            ri[k, c:c + 1, :] = rcv_ref[k:k + 1, c * D:(c + 1) * D]
    loads[0].wait()
    pl.semaphore_wait(barrier, len(everyone))

    def halo(s, d, n, to):
        return pltpu.make_async_remote_copy(
            src_ref=s, dst_ref=d, send_sem=sem_hs.at[n], recv_sem=sem_hr.at[n],
            device_id=to, device_id_type=MESH)

    def remote(s, d, n, to):
        return pltpu.make_async_remote_copy(
            src_ref=s, dst_ref=d, send_sem=sem_s.at[n], recv_sem=sem_r.at[n],
            device_id=to, device_id_type=MESH)

    outward = [halo(src.at[0], src.at[1], 0, up), halo(src.at[0], src.at[2], 1, after),
               halo(src.at[0], src.at[3], 2, before)]
    for c in outward:
        c.start()

    wi = wi_ref[...]
    w1, w2, w3 = wi[0:D, :], wi[D:2 * D, :], wi[2 * D:3 * D, :]
    wo = wo_ref[...]
    wn1, wn2 = ni_ref[0:D, :], ni_ref[D:2 * D, :]

    def receivers(k, _):
        for t in range(E // GT):
            cols = []
            for n in range(t * (GT // D), (t + 1) * (GT // D)):
                cols.append(spread(ri[k, n:n + 1, :]))
                rcol[rows_at(k * E + n * D, D), :] = cols[-1]
            inp[rows_at(k * E + t * GT, GT), D:2 * D] = mm2(tall_hot(cols), src[0]).astype(BF)
        return 0

    lax.fori_loop(0, K, receivers, 0)
    loads[1].wait()

    def senders(k, t):
        cols = [spread(si[k, n:n + 1, :]) for n in range(t * (GT // D), (t + 1) * (GT // D))]
        inp[rows_at(k * E + t * GT, GT), 0:D] = mm2(tall_hot(cols), src[k]).astype(BF)

    def hidden(k, t):
        rows = rows_at(k * E + t * GT, GT)
        u, h, d = norm_parts(mm2(inp[rows, :], wi))
        live = (lax.broadcasted_iota(jnp.int32, (GT, D), 0) + t * GT) < cnt_ref[k]
        U[rows, :] = u
        A[rows, :] = jnp.where(live, d, 0.0)
        hid[rows, :] = jnp.where(live, h, 0.0).astype(BF)

    tiles = [(k, t) for k in range(K) for t in range(E // GT)]
    for n, (k, t) in enumerate(tiles):
        if k and t == 0:
            outward[k - 1].wait()
        senders(k, t)
        if n:
            hidden(*tiles[n - 1])
    hidden(*tiles[-1])

    for m in range(N // ST):
        rows = rows_at(m * ST, ST)
        hi, lo = halves(mm2(receiver_hot(rcv_ref, m), hid[...]))
        t3[rows, 0:D] = hi
        t3[rows, D:2 * D] = lo
    loads[2].wait()
    incoming = (mm(t3[:, 0:D], wo) + mm(t3[:, D:2 * D], wo)).astype(BF)
    u, h, d = norm_parts(mm(src[0], wn1) + mm(incoming, wn2))
    ghv = gh[...]
    wg[6 * D:7 * D, :] = mm_tn(h.astype(BF), ghv)
    npg = norm_back(mm_nt(ghv, no_ref[...]) * d, u).astype(BF)
    wg[4 * D:5 * D, :] = mm_tn(src[0], npg)
    wg[5 * D:6 * D, :] = mm_tn(incoming, npg)
    wg[7 * D:8 * D, :] = jnp.zeros((D, D), F32)
    wt[...] = jnp.zeros((D, 4 * D), F32)
    hit_out[...] = ghv.astype(F32) + mm_nt(npg, wn1)
    hi, lo = halves(mm_nt(npg, wn2))
    t3[:, 0:D] = hi
    t3[:, D:2 * D] = lo
    loads[3].wait()

    def pull(k, t):
        base = k * E + t * GT
        rows = rows_at(base, GT)
        cols = [rcol[rows_at(base + n * D, D), :] for n in range(GT // D)]
        mg[rows, :] = (ge[rows, :].astype(F32)
                       + fold(mm(tall_hot(cols), t3[...]))).astype(BF)

    def chain(k, t):
        rows = rows_at(k * E + t * GT, GT)
        g[rows, :] = norm_back(mm_nt(mg[rows, :], wo) * A[rows, :], U[rows, :]).astype(BF)

    def weights(k):
        rows = rows_at(k * E, E)
        wt[:, 0:3 * D] += mm_tn(g[rows, :], inp[rows, :])
        wt[:, 3 * D:4 * D] += mm_tn(mg[rows, :], hid[rows, :])

    def meet_mate(q):
        send_a[q] = wg[rows_at(q * 2 * HALF + (1 - core) * HALF, HALF), :].astype(BF)
        c = remote(send_a.at[q], recv_a.at[q], q * SEMS, mate)
        c.start()
        return c

    def spread_plane(q, c):
        c.wait()
        own = wg[rows_at(q * 2 * HALF + core * HALF, HALF), :]
        send_b[q] = (own + recv_a[q].astype(F32)).astype(BF)
        copies = []
        for d, other in enumerate(plane, 1):
            piece = rows_at(((spot + d) % XY) * PIECE, PIECE)
            copies.append(remote(send_b.at[q, piece, :], recv_b.at[q, spot], q * SEMS + d, other))
            copies[-1].start()
        recv_b[q, spot] = send_b[q, rows_at(spot * PIECE, PIECE), :]
        return copies

    def spread_line(q, copies):
        for c in copies:
            c.wait()
        total = recv_b[q, 0].astype(F32)
        for j in range(1, XY):
            total = total + recv_b[q, j].astype(F32)
        send_c[q] = total.astype(BF)
        copies = []
        for d, other in enumerate(line, 1):
            copies.append(remote(send_c.at[q], recv_c.at[q, z], q * SEMS + XY + d, other))
            copies[-1].start()
        recv_c[q, z] = send_c[q]
        return copies

    def gather_plane(q, copies):
        for c in copies:
            c.wait()
        total = recv_c[q, 0].astype(F32)
        for j in range(1, LZ):
            total = total + recv_c[q, j].astype(F32)
        send_d[q] = (total * (1.0 / 256.0)).astype(BF)
        here = rows_at(q * 2 * HALF + core * HALF + spot * PIECE, PIECE)
        copies = []
        for d, other in enumerate(plane, 1):
            copies.append(remote(send_d.at[q], fin.at[here, :], q * SEMS + XY + LZ + d, other))
            copies[-1].start()
        fin[here, :] = send_d[q]
        return copies

    def gather_mate(q, copies):
        for c in copies:
            c.wait()
        mine = rows_at(q * 2 * HALF + core * HALF, HALF)
        c = remote(fin.at[mine, :], fin.at[mine, :], q * SEMS + XY + LZ, mate)
        c.start()
        return c

    early = meet_mate(1)
    for n, (k, t) in enumerate(tiles):
        pull(k, t)
        if n:
            chain(*tiles[n - 1])
        if k and t == 1:
            weights(k - 1)
        if n == 3:
            early = spread_plane(1, early)
    chain(*tiles[-1])
    weights(K - 1)
    for j in range(4):
        wg[j * D:(j + 1) * D, :] = wt[:, j * D:(j + 1) * D].T

    late = meet_mate(0)

    def give_back(k):
        for m in range(N // ST):
            rows = rows_at(m * ST, ST)
            s = mm2(scatter_hot(snd_ref, k, m), g[k * E:(k + 1) * E, :])
            bsend[k - 1, rows, :] = wide_nt(s, w1).astype(BF)
        return halo(bsend.at[k - 1], brecv.at[k - 1], 2 + k, (None, down, before, after)[k])

    homeward = [give_back(2)]
    late = spread_plane(0, late)
    homeward[0].start()
    homeward.append(give_back(3))
    homeward[1].start()
    early = spread_line(1, early)
    homeward.append(give_back(1))
    homeward[2].start()
    for m in range(N // ST):
        rows = rows_at(m * ST, ST)
        hit_out[rows, :] += wide_nt(mm2(scatter_hot(snd_ref, 0, m), g[0:E, :]), w1)
    late = spread_line(0, late)
    for m in range(N // ST):
        rows = rows_at(m * ST, ST)
        hi, lo = halves(mm2(receiver_hot(rcv_ref, m), g[...]))
        t3[rows, 0:D] = hi
        t3[rows, D:2 * D] = lo
    early = gather_plane(1, early)
    late = gather_plane(0, late)
    row = jnp.concatenate([w2, w2], axis=1)
    for m in range(N // ST):
        rows = rows_at(m * ST, ST)
        hit_out[rows, :] += mm_nt(t3[rows, :], jnp.concatenate([row, row], axis=0))[:, 0:D]
    for n in range(KE // GT):
        rows = rows_at(n * GT, GT)
        ebuf[rows, :] = (ge[rows, :].astype(F32) + mm_nt(g[rows, :], w3)).astype(BF)
    store = pltpu.make_async_copy(ebuf, edge_out, sem_in.at[4])
    store.start()
    early = gather_mate(1, early)
    late = gather_mate(0, late)
    for c in homeward:
        c.wait()
    hit_out[...] += (brecv[0].astype(F32) + brecv[1].astype(F32)) + brecv[2].astype(F32)
    early.wait()
    late.wait()
    store.wait()


def step_call(cnt, snd, rcv, hit, ef, gh, ge, wi, wo, ni, no):
    V = pl.BlockSpec(memory_space=pltpu.VMEM)
    H = pl.BlockSpec(memory_space=pl.ANY)
    sem = pltpu.SemaphoreType.DMA
    return pl.pallas_call(
        step_kernel,
        out_shape=(jax.ShapeDtypeStruct((N, D), F32), jax.ShapeDtypeStruct((KE, D), BF),
                   jax.ShapeDtypeStruct((8 * D, D), BF)),
        in_specs=[pl.BlockSpec(memory_space=pltpu.SMEM), V, V, H, H, H, H, V, V, V, V],
        out_specs=(V, H, V),
        scratch_shapes=[
            pltpu.VMEM((K, N, D), BF), pltpu.VMEM((KE, 3 * D), BF),
            pltpu.VMEM((N, D), BF), pltpu.VMEM((KE, D), BF),
            pltpu.VMEM((KE, D), jnp.int16), pltpu.VMEM((D, 4 * D), F32), pltpu.VMEM((KE, D), BF),
            pltpu.VMEM((KE, D), F32), pltpu.VMEM((KE, D), F32), pltpu.VMEM((KE, D), BF),
            pltpu.VMEM((KE, D), BF), pltpu.VMEM((KE, D), BF), pltpu.VMEM((N, 2 * D), BF),
            pltpu.VMEM((K, E // D, D), jnp.int32), pltpu.VMEM((K, E // D, D), jnp.int32),
            pltpu.VMEM((8 * D, D), F32),
            pltpu.VMEM((3, N, D), BF), pltpu.VMEM((3, N, D), BF),
            pltpu.VMEM((2, HALF, D), BF), pltpu.VMEM((2, HALF, D), BF), pltpu.VMEM((2, HALF, D), BF),
            pltpu.VMEM((2, XY, PIECE, D), BF), pltpu.VMEM((2, LZ, PIECE, D), BF),
            pltpu.VMEM((2, PIECE, D), BF), pltpu.VMEM((2, PIECE, D), BF),
            sem((5,)), sem((6,)), sem((6,)), sem((2 * SEMS,)), sem((2 * SEMS,)),
        ],
        compiler_params=pltpu.CompilerParams(
            vmem_limit_bytes=60 << 20, collective_id=0, has_side_effects=True),
        name="graph_step",
    )(cnt, snd, rcv, hit, ef, gh, ge, wi, wo, ni, no)


def finish_kernel(hits_in, edges_in, fin_in, hits, edges, g1, g2, g3, g4,
                  hbuf, ebuf, fbuf, wbuf, sem_i, sem_o):
    loads = [pltpu.make_async_copy(fin_in, fbuf, sem_i.at[0])]
    for k in range(K):
        part = pl.ds(k * E, E)
        loads.append(pltpu.make_async_copy(
            edges_in.at[part, :], ebuf.at[part, :], sem_i.at[k + 1]))
    loads.append(pltpu.make_async_copy(hits_in, hbuf, sem_i.at[5]))
    for c in loads:
        c.start()
    stores = []
    loads[0].wait()
    wbuf[...] = fbuf[...].astype(F32)
    first = 0
    for n, out in enumerate((g1, g2, g3, g4)):
        size = out.shape[0]
        stores.append(pltpu.make_async_copy(wbuf.at[pl.ds(first, size), :], out, sem_o.at[n]))
        stores[-1].start()
        first += size
    for k in range(K):
        part = pl.ds(k * E, E)
        loads[k + 1].wait()
        stores.append(pltpu.make_async_copy(ebuf.at[part, :], edges.at[part, :], sem_o.at[4 + k]))
        stores[-1].start()
    loads[5].wait()
    stores.append(pltpu.make_async_copy(hbuf, hits, sem_o.at[8]))
    stores[-1].start()
    for c in stores:
        c.wait()


def finish_call(hits, edges, fin):
    H = pl.BlockSpec(memory_space=pl.ANY)
    sem = pltpu.SemaphoreType.DMA
    shape = jax.ShapeDtypeStruct
    return pl.pallas_call(
        finish_kernel,
        out_shape=(shape((N, D), F32), shape((KE, D), BF), shape((3 * D, D), F32),
                   shape((D, D), F32), shape((2 * D, D), F32), shape((D, D), F32)),
        in_specs=[H, H, H],
        out_specs=(H,) * 6,
        scratch_shapes=[pltpu.VMEM((N, D), F32), pltpu.VMEM((KE, D), BF),
                        pltpu.VMEM((8 * D, D), BF), pltpu.VMEM((8 * D, D), F32),
                        sem((6,)), sem((9,))],
        compiler_params=pltpu.CompilerParams(vmem_limit_bytes=60 << 20),
        name="finish",
    )(hits, edges, fin)


def body(hit, ef, snd, rcv, cnt, gh, ge, wi, wo, ni, no):
    hits, edges, fin = step_call(
        cnt[0, 0], snd[0, 0], rcv[0, 0], hit[0, 0], ef[0, 0].reshape(KE, D),
        gh[0, 0], ge[0, 0].reshape(KE, D), wi, wo, ni, no)
    hits, edges, g1, g2, g3, g4 = finish_call(hits, edges, fin)
    return hits[None, None], edges.reshape(1, 1, K, E, D), g1, g2, g3, g4


def solution(mesh):
    two = P("layer", "phi", None, None)
    three = P("layer", "phi", None, None, None)
    return jax.shard_map(
        body, mesh=mesh,
        in_specs=(two, three, two, two, P("layer", "phi", None), two, three, P(), P(), P(), P()),
        out_specs=(two, three, P(), P(), P(), P()),
        check_vma=False,
    )
```

```python
import jax
import jax.numpy as jnp
from jax import lax
from jax.experimental import pallas as pl
from jax.experimental.pallas import tpu as pltpu
from jax.sharding import PartitionSpec as P

F32 = jnp.float32
BF = jnp.bfloat16
MESH = pl.DeviceIdType.MESH
N, E, D, K = 1024, 1024, 128, 4
KE = K * E
TE = 256
GT = 512
ST = 512
LZ, XY, HALF = 8, 16, 256
SEMS = 2 * XY + LZ
PIECE = HALF // XY


def mm(a, b):
    return jnp.dot(a, b, preferred_element_type=F32)


def mm2(a, b):
    return jnp.dot(a, jnp.concatenate([b, b], axis=1), preferred_element_type=F32)[:, 0:D]


def mm_nt(a, b):
    return lax.dot_general(a, b, (((1,), (1,)), ((), ())), preferred_element_type=F32)


def mm_tn(a, b):
    return lax.dot_general(a, b, (((0,), (0,)), ((), ())), preferred_element_type=F32)


def halves(x):
    hi = x.astype(BF)
    return hi, (x - hi.astype(F32)).astype(BF)


def wide_nt(x, w):
    both = jnp.concatenate(halves(x), axis=1)
    row = jnp.concatenate([w, w], axis=1)
    return mm_nt(both, jnp.concatenate([row, row], axis=0))[:, 0:D]


def fold(x):
    return x[:, 0:D] + x[:, D:2 * D]


def gather_hot(col):
    lane = lax.broadcasted_iota(jnp.int16, (D, D), 1)
    return jnp.concatenate(
        [jnp.where(col == lane + jnp.int16(j * D), BF(1), BF(0)) for j in range(N // D)], axis=1)


def spread(idx_row):
    return jnp.broadcast_to(idx_row, (D, D)).T.astype(jnp.int16)


def tall_hot(cols):
    return jnp.concatenate([gather_hot(c) for c in cols], axis=0)


def scatter_hot(idx_ref, k, m):
    ids = idx_ref[k:k + 1, :].astype(jnp.int16)
    io = lax.broadcasted_iota(jnp.int16, (ST, E), 0) + jnp.int16(m * ST)
    return jnp.where(jnp.broadcast_to(ids, (ST, E)) == io, BF(1), BF(0))


def receiver_hot(idx_ref, m):
    return jnp.concatenate([scatter_hot(idx_ref, k, m) for k in range(K)], axis=1)


def norm_parts(pre):
    mean = jnp.mean(pre, axis=-1, keepdims=True)
    c = pre - mean
    var = jnp.mean(c * c, axis=-1, keepdims=True)
    r = lax.rsqrt(var + 1e-5)
    u = c * r
    s = 0.5 + 0.5 * jnp.tanh(0.5 * u)
    h = u * s
    return u, h, r * (s + h * (1.0 - s))


def norm_back(w, u):
    return w - jnp.mean(w, axis=-1, keepdims=True) - u * jnp.mean(w * u, axis=-1, keepdims=True)


def rows_at(start, size):
    return pl.ds(pl.multiple_of(start, size), size)


def step_kernel(cnt_ref, snd_ref, rcv_ref, hit_any, ef_any, gh_any, ge_any,
                wi_ref, wo_ref, ni_ref, no_ref,
                hit_out, edge_out, fin,
                src, inp, gh, ge, rcol, wt, ebuf, A, U, hid, g, mg, t3, si, ri, wg,
                bsend, brecv, send_a, recv_a, send_b, recv_b, recv_c, send_c, send_d,
                sem_in, sem_hs, sem_hr, sem_s, sem_r):
    layer = lax.axis_index("layer")
    phi = lax.axis_index("phi")
    core = layer % 2
    spot = ((phi // 32) * 2 + layer // 2) * 4 + phi % 4
    z = (phi // 4) % 8

    def at(c, s, zz):
        y = s // 4
        return ((y % 2) * 2 + c, (y // 2) * 32 + zz * 4 + s % 4)

    up = ((layer + 1) % 4, phi)
    down = ((layer + 3) % 4, phi)
    after = (layer, (phi + 1) % 64)
    before = (layer, (phi + 63) % 64)
    mate = at(1 - core, spot, z)
    plane = [at(core, (spot + d) % XY, z) for d in range(1, XY)]
    line = [at(core, spot, (z + d) % LZ) for d in range(1, LZ)]
    everyone = [up, down, after, before, mate] + plane + line
    barrier = pltpu.get_barrier_semaphore()
    for other in everyone:
        pl.semaphore_signal(barrier, inc=1, device_id=other, device_id_type=MESH)
    loads = [
        pltpu.make_async_copy(hit_any, src.at[0], sem_in.at[0]),
        pltpu.make_async_copy(ef_any, inp.at[:, 2 * D:3 * D], sem_in.at[1]),
        pltpu.make_async_copy(gh_any, gh, sem_in.at[2]),
        pltpu.make_async_copy(ge_any, ge, sem_in.at[3]),
    ]
    for c in loads:
        c.start()
    pl.semaphore_wait(barrier, len(everyone))

    def halo(s, d, n, to):
        return pltpu.make_async_remote_copy(
            src_ref=s, dst_ref=d, send_sem=sem_hs.at[n], recv_sem=sem_hr.at[n],
            device_id=to, device_id_type=MESH)

    def remote(s, d, n, to):
        return pltpu.make_async_remote_copy(
            src_ref=s, dst_ref=d, send_sem=sem_s.at[n], recv_sem=sem_r.at[n],
            device_id=to, device_id_type=MESH)

    outward = [halo(hit_any, src.at[1], 0, up), halo(hit_any, src.at[2], 1, after),
               halo(hit_any, src.at[3], 2, before)]
    for c in outward:
        c.start()
    for k in range(K):
        for c in range(E // D):
            si[k, c:c + 1, :] = snd_ref[k:k + 1, c * D:(c + 1) * D]
            ri[k, c:c + 1, :] = rcv_ref[k:k + 1, c * D:(c + 1) * D]
    loads[0].wait()

    wi = wi_ref[...]
    w1, w2, w3 = wi[0:D, :], wi[D:2 * D, :], wi[2 * D:3 * D, :]
    wo = wo_ref[...]
    wn1, wn2 = ni_ref[0:D, :], ni_ref[D:2 * D, :]

    def receivers(k, _):
        for t in range(E // GT):
            cols = []
            for n in range(t * (GT // D), (t + 1) * (GT // D)):
                cols.append(spread(ri[k, n:n + 1, :]))
                rcol[rows_at(k * E + n * D, D), :] = cols[-1]
            inp[rows_at(k * E + t * GT, GT), D:2 * D] = mm2(tall_hot(cols), src[0]).astype(BF)
        return 0

    lax.fori_loop(0, K, receivers, 0)
    loads[1].wait()

    def senders(k, t):
        cols = [spread(si[k, n:n + 1, :]) for n in range(t * (GT // D), (t + 1) * (GT // D))]
        inp[rows_at(k * E + t * GT, GT), 0:D] = mm2(tall_hot(cols), src[k]).astype(BF)

    def hidden(k, t):
        rows = rows_at(k * E + t * GT, GT)
        u, h, d = norm_parts(mm2(inp[rows, :], wi))
        live = (lax.broadcasted_iota(jnp.int32, (GT, D), 0) + t * GT) < cnt_ref[k]
        U[rows, :] = u
        A[rows, :] = jnp.where(live, d, 0.0)
        hid[rows, :] = jnp.where(live, h, 0.0).astype(BF)

    tiles = [(k, t) for k in range(K) for t in range(E // GT)]
    for n, (k, t) in enumerate(tiles):
        if k and t == 0:
            outward[k - 1].wait()
        senders(k, t)
        if n:
            hidden(*tiles[n - 1])
    hidden(*tiles[-1])

    for m in range(N // ST):
        rows = rows_at(m * ST, ST)
        hi, lo = halves(mm2(receiver_hot(rcv_ref, m), hid[...]))
        t3[rows, 0:D] = hi
        t3[rows, D:2 * D] = lo
    loads[2].wait()
    incoming = (mm(t3[:, 0:D], wo) + mm(t3[:, D:2 * D], wo)).astype(BF)
    u, h, d = norm_parts(mm(src[0], wn1) + mm(incoming, wn2))
    ghv = gh[...]
    wg[6 * D:7 * D, :] = mm_tn(h.astype(BF), ghv)
    npg = norm_back(mm_nt(ghv, no_ref[...]) * d, u).astype(BF)
    wg[4 * D:5 * D, :] = mm_tn(src[0], npg)
    wg[5 * D:6 * D, :] = mm_tn(incoming, npg)
    wg[7 * D:8 * D, :] = jnp.zeros((D, D), F32)
    wt[...] = jnp.zeros((D, 4 * D), F32)
    hit_out[...] = ghv.astype(F32) + mm_nt(npg, wn1)
    hi, lo = halves(mm_nt(npg, wn2))
    t3[:, 0:D] = hi
    t3[:, D:2 * D] = lo
    loads[3].wait()

    def pull(k, t):
        base = k * E + t * GT
        rows = rows_at(base, GT)
        cols = [rcol[rows_at(base + n * D, D), :] for n in range(GT // D)]
        mg[rows, :] = (ge[rows, :].astype(F32)
                       + fold(mm(tall_hot(cols), t3[...]))).astype(BF)

    def chain(k, t):
        rows = rows_at(k * E + t * GT, GT)
        g[rows, :] = norm_back(mm_nt(mg[rows, :], wo) * A[rows, :], U[rows, :]).astype(BF)

    def weights(k):
        rows = rows_at(k * E, E)
        wt[:, 0:3 * D] += mm_tn(g[rows, :], inp[rows, :])
        wt[:, 3 * D:4 * D] += mm_tn(mg[rows, :], hid[rows, :])

    def meet_mate(q):
        send_a[q] = wg[rows_at(q * 2 * HALF + (1 - core) * HALF, HALF), :].astype(BF)
        c = remote(send_a.at[q], recv_a.at[q], q * SEMS, mate)
        c.start()
        return c

    def spread_plane(q, c):
        c.wait()
        own = wg[rows_at(q * 2 * HALF + core * HALF, HALF), :]
        send_b[q] = (own + recv_a[q].astype(F32)).astype(BF)
        copies = []
        for d, other in enumerate(plane, 1):
            piece = rows_at(((spot + d) % XY) * PIECE, PIECE)
            copies.append(remote(send_b.at[q, piece, :], recv_b.at[q, spot], q * SEMS + d, other))
            copies[-1].start()
        recv_b[q, spot] = send_b[q, rows_at(spot * PIECE, PIECE), :]
        return copies

    def spread_line(q, copies):
        for c in copies:
            c.wait()
        total = recv_b[q, 0].astype(F32)
        for j in range(1, XY):
            total = total + recv_b[q, j].astype(F32)
        send_c[q] = total.astype(BF)
        copies = []
        for d, other in enumerate(line, 1):
            copies.append(remote(send_c.at[q], recv_c.at[q, z], q * SEMS + XY + d, other))
            copies[-1].start()
        recv_c[q, z] = send_c[q]
        return copies

    def gather_plane(q, copies):
        for c in copies:
            c.wait()
        total = recv_c[q, 0].astype(F32)
        for j in range(1, LZ):
            total = total + recv_c[q, j].astype(F32)
        send_d[q] = (total * (1.0 / 256.0)).astype(BF)
        here = rows_at(q * 2 * HALF + core * HALF + spot * PIECE, PIECE)
        copies = []
        for d, other in enumerate(plane, 1):
            copies.append(remote(send_d.at[q], fin.at[here, :], q * SEMS + XY + LZ + d, other))
            copies[-1].start()
        fin[here, :] = send_d[q]
        return copies

    def gather_mate(q, copies):
        for c in copies:
            c.wait()
        mine = rows_at(q * 2 * HALF + core * HALF, HALF)
        c = remote(fin.at[mine, :], fin.at[mine, :], q * SEMS + XY + LZ, mate)
        c.start()
        return c

    early = meet_mate(1)
    for n, (k, t) in enumerate(tiles):
        pull(k, t)
        if n:
            chain(*tiles[n - 1])
        if k and t == 1:
            weights(k - 1)
        if n == 3:
            early = spread_plane(1, early)
    chain(*tiles[-1])
    weights(K - 1)
    for j in range(4):
        wg[j * D:(j + 1) * D, :] = wt[:, j * D:(j + 1) * D].T

    late = meet_mate(0)

    def give_back(k):
        for m in range(N // ST):
            rows = rows_at(m * ST, ST)
            s = mm2(scatter_hot(snd_ref, k, m), g[k * E:(k + 1) * E, :])
            bsend[k - 1, rows, :] = wide_nt(s, w1).astype(BF)
        return halo(bsend.at[k - 1], brecv.at[k - 1], 2 + k, (None, down, before, after)[k])

    homeward = [give_back(2)]
    late = spread_plane(0, late)
    homeward[0].start()
    homeward.append(give_back(3))
    homeward[1].start()
    early = spread_line(1, early)
    homeward.append(give_back(1))
    homeward[2].start()
    for m in range(N // ST):
        rows = rows_at(m * ST, ST)
        hit_out[rows, :] += wide_nt(mm2(scatter_hot(snd_ref, 0, m), g[0:E, :]), w1)
    late = spread_line(0, late)
    for m in range(N // ST):
        rows = rows_at(m * ST, ST)
        hi, lo = halves(mm2(receiver_hot(rcv_ref, m), g[...]))
        t3[rows, 0:D] = hi
        t3[rows, D:2 * D] = lo
    early = gather_plane(1, early)
    late = gather_plane(0, late)
    row = jnp.concatenate([w2, w2], axis=1)
    for m in range(N // ST):
        rows = rows_at(m * ST, ST)
        hit_out[rows, :] += mm_nt(t3[rows, :], jnp.concatenate([row, row], axis=0))[:, 0:D]
    for n in range(KE // GT):
        rows = rows_at(n * GT, GT)
        ebuf[rows, :] = (ge[rows, :].astype(F32) + mm_nt(g[rows, :], w3)).astype(BF)
    store = pltpu.make_async_copy(ebuf, edge_out, sem_in.at[4])
    store.start()
    early = gather_mate(1, early)
    late = gather_mate(0, late)
    for c in homeward:
        c.wait()
    hit_out[...] += (brecv[0].astype(F32) + brecv[1].astype(F32)) + brecv[2].astype(F32)
    early.wait()
    late.wait()
    store.wait()


def step_call(cnt, snd, rcv, hit, ef, gh, ge, wi, wo, ni, no):
    V = pl.BlockSpec(memory_space=pltpu.VMEM)
    H = pl.BlockSpec(memory_space=pl.ANY)
    sem = pltpu.SemaphoreType.DMA
    return pl.pallas_call(
        step_kernel,
        out_shape=(jax.ShapeDtypeStruct((N, D), F32), jax.ShapeDtypeStruct((KE, D), BF),
                   jax.ShapeDtypeStruct((8 * D, D), BF)),
        in_specs=[pl.BlockSpec(memory_space=pltpu.SMEM), V, V, H, H, H, H, V, V, V, V],
        out_specs=(V, H, V),
        scratch_shapes=[
            pltpu.VMEM((K, N, D), BF), pltpu.VMEM((KE, 3 * D), BF),
            pltpu.VMEM((N, D), BF), pltpu.VMEM((KE, D), BF),
            pltpu.VMEM((KE, D), jnp.int16), pltpu.VMEM((D, 4 * D), F32), pltpu.VMEM((KE, D), BF),
            pltpu.VMEM((KE, D), F32), pltpu.VMEM((KE, D), F32), pltpu.VMEM((KE, D), BF),
            pltpu.VMEM((KE, D), BF), pltpu.VMEM((KE, D), BF), pltpu.VMEM((N, 2 * D), BF),
            pltpu.VMEM((K, E // D, D), jnp.int32), pltpu.VMEM((K, E // D, D), jnp.int32),
            pltpu.VMEM((8 * D, D), F32),
            pltpu.VMEM((3, N, D), BF), pltpu.VMEM((3, N, D), BF),
            pltpu.VMEM((2, HALF, D), BF), pltpu.VMEM((2, HALF, D), BF), pltpu.VMEM((2, HALF, D), BF),
            pltpu.VMEM((2, XY, PIECE, D), BF), pltpu.VMEM((2, LZ, PIECE, D), BF),
            pltpu.VMEM((2, PIECE, D), BF), pltpu.VMEM((2, PIECE, D), BF),
            sem((5,)), sem((6,)), sem((6,)), sem((2 * SEMS,)), sem((2 * SEMS,)),
        ],
        compiler_params=pltpu.CompilerParams(
            vmem_limit_bytes=60 << 20, collective_id=0, has_side_effects=True),
        name="graph_step",
    )(cnt, snd, rcv, hit, ef, gh, ge, wi, wo, ni, no)


def finish_kernel(hits_in, edges_in, fin_in, hits, edges, g1, g2, g3, g4,
                  hbuf, ebuf, fbuf, wbuf, sem_i, sem_o):
    loads = [pltpu.make_async_copy(fin_in, fbuf, sem_i.at[0])]
    for k in range(K):
        part = pl.ds(k * E, E)
        loads.append(pltpu.make_async_copy(
            edges_in.at[part, :], ebuf.at[part, :], sem_i.at[k + 1]))
    loads.append(pltpu.make_async_copy(hits_in, hbuf, sem_i.at[5]))
    for c in loads:
        c.start()
    stores = []
    loads[0].wait()
    wbuf[...] = fbuf[...].astype(F32)
    first = 0
    for n, out in enumerate((g1, g2, g3, g4)):
        size = out.shape[0]
        stores.append(pltpu.make_async_copy(wbuf.at[pl.ds(first, size), :], out, sem_o.at[n]))
        stores[-1].start()
        first += size
    for k in range(K):
        part = pl.ds(k * E, E)
        loads[k + 1].wait()
        stores.append(pltpu.make_async_copy(ebuf.at[part, :], edges.at[part, :], sem_o.at[4 + k]))
        stores[-1].start()
    loads[5].wait()
    stores.append(pltpu.make_async_copy(hbuf, hits, sem_o.at[8]))
    stores[-1].start()
    for c in stores:
        c.wait()


def finish_call(hits, edges, fin):
    H = pl.BlockSpec(memory_space=pl.ANY)
    sem = pltpu.SemaphoreType.DMA
    shape = jax.ShapeDtypeStruct
    return pl.pallas_call(
        finish_kernel,
        out_shape=(shape((N, D), F32), shape((KE, D), BF), shape((3 * D, D), F32),
                   shape((D, D), F32), shape((2 * D, D), F32), shape((D, D), F32)),
        in_specs=[H, H, H],
        out_specs=(H,) * 6,
        scratch_shapes=[pltpu.VMEM((N, D), F32), pltpu.VMEM((KE, D), BF),
                        pltpu.VMEM((8 * D, D), BF), pltpu.VMEM((8 * D, D), F32),
                        sem((6,)), sem((9,))],
        compiler_params=pltpu.CompilerParams(vmem_limit_bytes=60 << 20),
        name="finish",
    )(hits, edges, fin)


def body(hit, ef, snd, rcv, cnt, gh, ge, wi, wo, ni, no):
    hits, edges, fin = step_call(
        cnt[0, 0], snd[0, 0], rcv[0, 0], hit[0, 0], ef[0, 0].reshape(KE, D),
        gh[0, 0], ge[0, 0].reshape(KE, D), wi, wo, ni, no)
    hits, edges, g1, g2, g3, g4 = finish_call(hits, edges, fin)
    return hits[None, None], edges.reshape(1, 1, K, E, D), g1, g2, g3, g4


def solution(mesh):
    two = P("layer", "phi", None, None)
    three = P("layer", "phi", None, None, None)
    return jax.shard_map(
        body, mesh=mesh,
        in_specs=(two, three, two, two, P("layer", "phi", None), two, three, P(), P(), P(), P()),
        out_specs=(two, three, P(), P(), P(), P()),
        check_vma=False,
    )
```
